256 devices in a mesh: lat: 8 (over x, y_hi), lon: 32 (over y_lo, z, core).
Axes of the slice: x: 4, y: 4 (y_hi: 2, y_lo: 2; y = y_hi * 2 + y_lo), z: 8, core: 2. Of those that a mesh axis runs over, the one named last changes fastest.
Arguments:
- tracers: float32 [128, 1440, 1536], P('lat', 'lon'), may hold values from 0.05 to 9, as said below
- winds: float32 [128, 1440, 32], P('lat', 'lon'), may hold values from -0.16 to 0.16
- row_mask: int32 [128], P('lat'), may hold values from 0 to 1, as said below
- coag_rate: float32 [16], replicated, may hold values from 0.05 to 0.3
- growth_rate: float32 [16], replicated, may hold values from 0.05 to 0.3
Outputs:
- updated: float32 [128, 1440, 1536], P('lat', 'lon')
The draws below stay inside these ranges and needn't reach their ends.
Inputs may be any that keep to these rules, and one draw needn't show every extreme that they name: `tracers`: per cell, mode and level the six channels are M_k = N exp(k mu + k^2 s^2 / 2), k = 0..5, with N in 0.3 to 3, mu in -0.5 to -0.2 and s in 0.25 to 0.4. `row_mask`: 1 on the first K rows (those nearest the pole) and 0 elsewhere, with 16 <= K <= 48.
All inputs are finite; a program needn't handle non-finite values.
Results may differ from the reference program's by a relative error of at most 0.00005.
Values sent between devices are 32-bit elements; how exact they have to be, the bound alone decides.
A program may use at most 128 MiB of HBM per device.

```python
import math
import jax
import jax.numpy as jnp
from jax import lax

NLON = 1440
GLOBE_ROWS = 720
LEV = 16
MODES = 16
MOMENTS = 6
NLAT = 128


def draw_tracers(key, part):
    key_count, key_centre, key_spread = jax.random.split(jax.random.fold_in(key, 11), 3)
    cells = (NLAT, NLON, MODES * LEV)
    amount = jnp.exp(jax.random.uniform(key_count, cells, jnp.float32, math.log(0.5), math.log(2.0)))
    centre = jax.random.uniform(key_centre, cells, jnp.float32, -0.45, -0.25)
    spread = jax.random.uniform(key_spread, cells, jnp.float32, 0.25, 0.38)
    pieces = [amount * jnp.exp(degree * centre + 0.5 * degree * degree * spread * spread) for degree in range(MOMENTS)]
    return jnp.concatenate(pieces, axis=2).astype(jnp.float32)


def draw_row_mask(key, part):
    cutoff = jax.random.randint(jax.random.fold_in(key, 5), (), NLAT // 8, 3 * NLAT // 8 + 1)
    places = jnp.arange(NLAT, dtype=jnp.int32)
    return (places < cutoff).astype(jnp.int32)


def block_scale(key, extent, shards, least, largest):
    gain, own = 1.0, jax.random.fold_in(key, 6)
    for position, blocks in shards:
        draws = jnp.exp(jax.random.uniform(jax.random.fold_in(own, position), (blocks,), jnp.float32, least / len(shards), largest / len(shards)))
        gain = gain * jnp.repeat(draws, extent[position] // blocks).reshape([-1 if axis == position else 1 for axis in range(len(extent))])
    return gain


def setup_inputs(seed: int = 0) -> dict:
    key_list = jax.random.split(jax.random.key(seed), 6)
    return {
        "tracers": draw_tracers(jax.random.fold_in(key_list[5], 71), 0),
        "winds": jnp.clip(jax.random.uniform(key_list[1], (NLAT, NLON, 2 * LEV), jnp.float32, -0.16, 0.16) * block_scale(key_list[1], (NLAT, NLON, 2 * LEV), ((0, 8), (1, 32)), -0.4, 0.0), -0.16, 0.16),
        "row_mask": draw_row_mask(jax.random.fold_in(key_list[5], 71), 0),
        "coag_rate": jnp.clip(jnp.exp(jax.random.uniform(key_list[3], (MODES,), jnp.float32, math.log(0.05), math.log(0.3))), 0.05, 0.3),
        "growth_rate": jnp.clip(jnp.exp(jax.random.uniform(key_list[4], (MODES,), jnp.float32, math.log(0.05), math.log(0.3))), 0.05, 0.3),
    }


CUT_COSINE = math.cos(math.pi / 4.0)

def row_angles(places):
    return (-90.0 + 180.0 * (places.astype(jnp.float32) + 0.5) / GLOBE_ROWS) * (math.pi / 180.0)

def damping(angles, length):
    waves = jnp.arange(length // 2 + 1, dtype=jnp.float32)
    sines = jnp.sin(waves * (math.pi / length))
    cosines = jnp.cos(angles)[:, None]
    return cosines / jnp.maximum(CUT_COSINE * sines[None, :], cosines)

def moment_sources(moments, coag, growth):
    zeroth, first, second, third, fourth, fifth = moments
    alpha_zero = first / zeroth
    sigma_one = second - alpha_zero * first
    sigma_two = third - alpha_zero * second
    sigma_three = fourth - alpha_zero * third
    sigma_four = fifth - alpha_zero * fourth
    alpha_one = sigma_two / sigma_one - first / zeroth
    beta_one = sigma_one / zeroth
    upper_two = sigma_three - alpha_one * sigma_two - beta_one * second
    upper_three = sigma_four - alpha_one * sigma_three - beta_one * third
    alpha_two = upper_three / upper_two - sigma_two / sigma_one
    beta_two = upper_two / sigma_one
    link_one = jnp.sqrt(beta_one)
    link_two = jnp.sqrt(beta_two)
    centre = (alpha_zero + alpha_one + alpha_two) / 3.0
    shift_zero = alpha_zero - centre
    shift_one = alpha_one - centre
    shift_two = alpha_two - centre
    radius = jnp.sqrt((shift_zero * shift_zero + shift_one * shift_one + shift_two * shift_two + 2.0 * (beta_one + beta_two)) / 6.0)
    scaled_zero = shift_zero / radius
    scaled_one = shift_one / radius
    scaled_two = shift_two / radius
    ratio_one = beta_one / (radius * radius)
    ratio_two = beta_two / (radius * radius)
    half_det = 0.5 * (scaled_zero * (scaled_one * scaled_two - ratio_two) - ratio_one * scaled_two)
    angle = jnp.arccos(jnp.clip(half_det, -1.0, 1.0)) / 3.0
    top_node = centre + 2.0 * radius * jnp.cos(angle)
    low_node = centre + 2.0 * radius * jnp.cos(angle + 2.0 * math.pi / 3.0)
    mid_node = 3.0 * centre - top_node - low_node
    abscissae = (top_node, mid_node, low_node)
    weights = []
    for node in abscissae:
        poly_one = (node - alpha_zero) / link_one
        poly_two = ((node - alpha_one) * poly_one - link_one) / link_two
        weights.append(zeroth / (1.0 + poly_one * poly_one + poly_two * poly_two))
    volumes = [node * node * node for node in abscissae]
    results = []
    for degree in range(6):
        merged = jnp.zeros_like(zeroth)
        for source in range(3):
            for target in range(3):
                joined = volumes[source] + volumes[target]
                change = jnp.exp(degree / 3.0 * jnp.log(joined)) - abscissae[source] ** degree - abscissae[target] ** degree
                merged = merged + weights[source] * weights[target] * joined * change
        growth_sum = jnp.zeros_like(zeroth)
        if degree > 0:
            for source in range(3):
                growth_sum = growth_sum + weights[source] * abscissae[source] ** (degree - 1) / (1.0 + abscissae[source])
            growth_sum = degree * growth * growth_sum
        results.append(moments[degree] + 0.5 * coag * merged + growth_sum)
    return tuple(results)

def polar_filter(winds, row_mask):
    factor = damping(row_angles(jnp.arange(NLAT, dtype=jnp.int32)), NLON)
    spectrum = jnp.fft.rfft(winds, axis=1)
    smooth = jnp.fft.irfft(spectrum * factor[:, :, None], n=NLON, axis=1).astype(jnp.float32)
    return jnp.where(row_mask[:, None, None] > 0, smooth, winds)

def advect(fields, zonal, merid):
    east_value = jnp.roll(fields, -1, axis=1)
    east_wind = jnp.roll(zonal, -1, axis=1)
    zonal_speed = 0.5 * (zonal + east_wind)
    flux_east = jnp.maximum(zonal_speed, 0.0) * fields + jnp.minimum(zonal_speed, 0.0) * east_value
    flux_west = jnp.roll(flux_east, 1, axis=1)
    zero_row = jnp.zeros_like(fields[:1])
    north_value = jnp.concatenate([fields[1:], zero_row], axis=0)
    north_wind = jnp.concatenate([merid[1:], zero_row], axis=0)
    places = jnp.arange(NLAT, dtype=jnp.int32)
    open_face = (places < NLAT - 1).astype(jnp.float32)[:, None, None]
    merid_speed = 0.5 * (merid + north_wind)
    flux_north = (jnp.maximum(merid_speed, 0.0) * fields + jnp.minimum(merid_speed, 0.0) * north_value) * open_face
    flux_south = jnp.concatenate([zero_row, flux_north[:-1]], axis=0)
    return fields - (flux_east - flux_west) - (flux_north - flux_south)

def reference(tracers, winds, row_mask, coag_rate, growth_rate):
    filtered = polar_filter(winds, row_mask)
    zonal = jnp.tile(filtered[:, :, :LEV], (1, 1, MODES))
    merid = jnp.tile(filtered[:, :, LEV:], (1, 1, MODES))
    block_width = MODES * LEV
    advected = [advect(tracers[:, :, degree * block_width:(degree + 1) * block_width], zonal, merid) for degree in range(MOMENTS)]
    coag = jnp.repeat(coag_rate, LEV)
    growth = jnp.repeat(growth_rate, LEV)

    def per_row(row_moments):
        return moment_sources(row_moments, coag, growth)
    updated = lax.map(per_row, tuple(advected))
    return jnp.concatenate(updated, axis=2)
```

```python
import functools
import math

import jax
import jax.numpy as jnp
import numpy as np
from jax import lax
from jax.experimental import pallas as pl
from jax.experimental.pallas import tpu as pltpu
from jax.sharding import PartitionSpec as P

NLON = 1440
GLOBE_ROWS = 720
LEV = 16
MODES = 16
MOMENTS = 6
FILTER_ROWS = 48
MESH = pl.DeviceIdType.MESH

POLY = (
    0.5000000260258313,
    0.577346917369578,
    -0.11103851124670026,
    0.052841409139758516,
    -0.03023539756350864,
    0.016047280362516254,
    -0.0060893456734267045,
    0.0011276362373084019,
)


def filter_lines(sectors, cols):
    rows = np.arange(FILTER_ROWS)
    angles = (-90.0 + 180.0 * (rows + 0.5) / GLOBE_ROWS) * (math.pi / 180.0)
    cosines = np.cos(angles)[:, None]
    sines = np.sin(np.arange(NLON // 2 + 1) * (math.pi / NLON))[None, :]
    factor = cosines / np.maximum(math.cos(math.pi / 4.0) * sines, cosines)
    kernel = np.fft.irfft(factor, n=NLON, axis=1)
    lane = np.arange(128)
    shift = np.where(lane < 64, lane, lane - 128)
    place = (cols * np.arange(sectors)[:, None] - 1 + shift[None, :]) % NLON
    return kernel[:, place].astype(np.float32)


def split_two(x):
    high = x.astype(jnp.bfloat16)
    return high, (x - high.astype(jnp.float32)).astype(jnp.bfloat16)


def nodes_of(moments):
    m0, m1, m2, m3, m4, m5 = moments
    inv0 = 1.0 / m0
    a0 = m1 * inv0
    s1 = m2 - a0 * m1
    s2 = m3 - a0 * m2
    s3 = m4 - a0 * m3
    s4 = m5 - a0 * m4
    inv1 = 1.0 / s1
    r21 = s2 * inv1
    a1 = r21 - a0
    b1 = s1 * inv0
    t2 = s3 - a1 * s2 - b1 * m2
    t3 = s4 - a1 * s3 - b1 * m3
    r32 = t3 * (1.0 / t2)
    a2 = r32 - r21
    b2 = t2 * inv1
    c = r32 * (1.0 / 3.0)
    g0, g1, g2 = a0 - c, a1 - c, a2 - c
    p2 = (g0 * g0 + g1 * g1 + g2 * g2) * (1.0 / 6.0) + (b1 + b2) * (1.0 / 3.0)
    inv_p = lax.rsqrt(p2)
    p = p2 * inv_p
    det = g0 * (g1 * g2 - b2) - b1 * g2
    h = jnp.clip((0.5 * det) * (inv_p * inv_p * inv_p), -1.0, 1.0)
    u = jnp.sqrt(0.5 + 0.5 * h)
    y = POLY[-1] * u + POLY[-2]
    for coef in POLY[-3::-1]:
        y = y * u + coef
    s = jnp.sqrt(jnp.maximum(0.75 - 0.75 * (y * y), 0.0))
    py, ps = p * y, p * s
    q = c - py
    return (c + 2.0 * py, q + 2.0 * ps, q - 2.0 * ps), (a0, a1, b1, b2, t2)


def moment_sources(moments, half_coag, growth):
    xs, (a0, a1, b1, b2, t2) = nodes_of(moments)
    ws, hs = [], []
    for x in xs:
        y = x - a0
        z = (x - a1) * y - b1
        den = b2 * (b1 + y * y) + z * z
        above = 1.0 + x
        share = t2 / (den * above)
        ws.append(share * above)
        hs.append(share * growth)
    vs = [x * x * x for x in xs]
    cw = [w * half_coag for w in ws]
    dia = [cw[i] * ws[i] * vs[i] for i in range(3)]
    off, roots = [], []
    for i, j in ((0, 1), (0, 2), (1, 2)):
        joined = vs[i] + vs[j]
        roots.append(jnp.exp(jnp.log(joined) * (1.0 / 3.0)))
        off.append(2.0 * cw[i] * ws[j] * joined)
    ends = [off[0] + off[1], off[0] + off[2], off[1] + off[2]]
    out = [moments[0] - (2.0 * (dia[0] + dia[1] + dia[2]) + (off[0] + off[1] + off[2]))]
    ax = [dia[i] * xs[i] for i in range(3)]
    ex = [ends[i] * xs[i] for i in range(3)]
    for k in range(1, MOMENTS):
        twin = 2.0 * 2.0 ** (k / 3.0) - 4.0
        off = [off[i] * roots[i] for i in range(3)]
        total = moments[k] + (off[0] + off[1] + off[2])
        terms = [twin * ax[i] - ex[i] + float(k) * hs[i] for i in range(3)]
        out.append(total + (terms[0] + terms[1] + terms[2]))
        if k < MOMENTS - 1:
            ax = [ax[i] * xs[i] for i in range(3)]
            ex = [ex[i] * xs[i] for i in range(3)]
            hs = [hs[i] * xs[i] for i in range(3)]
    return out


def kernel(
    bands, sectors, lines_ref, mask_ref, coag_ref, growth_ref, winds_ref, tracers_ref, out_ref,
    line_buf, wsend, wrecv, fsend, frecv, wide_h, wide_l, table_h, table_l, turn, coefs, rates,
    tbuf, obuf, south_buf, north_buf,
    line_sem, load_sem, store_sem, w_send, w_recv, f_send, f_recv, edge_send, edge_recv, v_send, v_recv,
):
    band, me = lax.axis_index("lat"), lax.axis_index("lon")
    north, south = lax.rem(band + 1, bands), lax.rem(band + bands - 1, bands)
    east, west = lax.rem(me + 1, sectors), lax.rem(me + sectors - 1, sectors)
    rows, channels, cols = winds_ref.shape
    width = tracers_ref.shape[-1]
    octets = rows // 8
    lane = lax.broadcasted_iota(jnp.int32, (8, 128), 1)
    sub = lax.broadcasted_iota(jnp.int32, (8, 128), 0)
    low = lane < 64

    barrier = pltpu.get_barrier_semaphore()

    def greet(k, carry):
        pl.semaphore_signal(barrier, inc=1, device_id=(band, lax.rem(me + k, sectors)), device_id_type=MESH)
        return carry

    lax.fori_loop(1, sectors, greet, 0)
    for other in (north, south):
        pl.semaphore_signal(barrier, inc=1, device_id=(other, me), device_id_type=MESH)

    unit_row = lax.div(me, 2)
    line = jnp.minimum(band * rows + unit_row, FILTER_ROWS - 1)
    line_copy = pltpu.make_async_copy(lines_ref.at[line], line_buf, line_sem)
    line_copy.start()
    load = pltpu.make_async_copy(tracers_ref, tbuf.at[pl.ds(1, cols)], load_sem)
    load.start()

    for unit in range(2 * rows):
        wsend[unit] = jnp.zeros((8, 128), jnp.float32)
        for g in range(2):
            start = 16 * (unit % 2) + 8 * g
            wsend[unit, :, 64 * g : 64 * g + cols] = winds_ref[unit // 2, start : start + 8, :]
    for half in range(2):
        c = jnp.zeros((8, 128), jnp.float32)
        g = jnp.zeros((8, 128), jnp.float32)
        for mode in range(8):
            here = lax.div(lane, LEV) == mode
            c = jnp.where(here, 0.5 * coag_ref[8 * half + mode], c)
            g = jnp.where(here, growth_ref[8 * half + mode], g)
        rates[0, half] = c
        rates[1, half] = g

    line_copy.wait()
    filtered = mask_ref[unit_row] > 0
    for k in range(sectors):
        parts = []
        for side in range(2):
            e = (side - k) % sectors
            values = line_buf[e : e + 1, :]
            unit_line = jnp.zeros((1, 128), jnp.float32)
            for x in range(128):
                if (cols * e - 1 + (x if x < 64 else x - 128)) % NLON == 0:
                    unit_line = jnp.where(lax.broadcasted_iota(jnp.int32, (1, 128), 1) == x, 1.0, unit_line)
            values = jnp.where(filtered, values, unit_line)
            parts.append(pltpu.roll(jnp.broadcast_to(values, (64, 128)), 64 * side, 1, stride=1, stride_axis=0))
        left = lax.broadcasted_iota(jnp.int32, (64, 128), 1) < 64
        high, rest = split_two(jnp.where(left, parts[0], parts[1]))
        table_h[64 * k : 64 * k + 64, :] = high
        table_l[64 * k : 64 * k + 64, :] = rest

    pl.semaphore_wait(barrier, sectors + 1)

    def wind_copy(k):
        other = lax.rem(me + k, sectors)
        return pltpu.make_async_remote_copy(
            src_ref=wsend.at[other], dst_ref=wrecv.at[me], send_sem=w_send.at[other], recv_sem=w_recv.at[me],
            device_id=(band, other), device_id_type=MESH,
        )

    def wind_start(k, carry):
        wind_copy(k).start()
        return carry

    lax.fori_loop(1, sectors, wind_start, 0)
    wrecv[me] = wsend[me]

    edges = [
        pltpu.make_async_remote_copy(
            src_ref=tracers_ref.at[cols - 1], dst_ref=tbuf.at[0], send_sem=edge_send.at[0], recv_sem=edge_recv.at[0],
            device_id=(band, east), device_id_type=MESH,
        ),
        pltpu.make_async_remote_copy(
            src_ref=tracers_ref.at[0], dst_ref=tbuf.at[cols + 1], send_sem=edge_send.at[1], recv_sem=edge_recv.at[1],
            device_id=(band, west), device_id_type=MESH,
        ),
        pltpu.make_async_remote_copy(
            src_ref=tracers_ref.at[:, pl.ds(rows - 1, 1), :], dst_ref=south_buf, send_sem=edge_send.at[2],
            recv_sem=edge_recv.at[2], device_id=(north, me), device_id_type=MESH,
        ),
        pltpu.make_async_remote_copy(
            src_ref=tracers_ref.at[:, pl.ds(0, 1), :], dst_ref=north_buf, send_sem=edge_send.at[3],
            recv_sem=edge_recv.at[3], device_id=(south, me), device_id_type=MESH,
        ),
    ]
    for copy in edges:
        copy.start()

    def wind_wait(k, carry):
        other = lax.rem(me + k, sectors)
        pltpu.make_async_remote_copy(
            src_ref=wsend.at[me], dst_ref=wrecv.at[other], send_sem=w_send.at[other], recv_sem=w_recv.at[other],
            device_id=(band, other), device_id_type=MESH,
        ).wait_recv()
        return carry

    lax.fori_loop(1, sectors, wind_wait, 0)

    pairs = sectors // 2
    for q in range(pairs):
        one, two = wrecv[2 * q], wrecv[2 * q + 1]
        block = jnp.concatenate(
            [jnp.where(low, one, pltpu.roll(two, 64, 1)), jnp.where(low, pltpu.roll(one, 64, 1), two)], axis=0
        )
        high, rest = split_two(block)
        for p in range(pairs):
            at = 128 * ((q - p) % pairs)
            wide_h[16 * p : 16 * p + 16, at : at + 128] = high
            wide_l[16 * p : 16 * p + 16, at : at + 128] = rest
    dot = functools.partial(jnp.dot, preferred_element_type=jnp.float32)
    smooth = dot(wide_h[...], table_h[...]) + (dot(wide_l[...], table_h[...]) + dot(wide_h[...], table_l[...]))
    for p in range(pairs):
        one, two = smooth[16 * p : 16 * p + 8, :], smooth[16 * p + 8 : 16 * p + 16, :]
        fsend[2 * p] = jnp.where(low, one, pltpu.roll(two, 64, 1))
        fsend[2 * p + 1] = jnp.where(low, pltpu.roll(one, 64, 1), two)

    def back_start(k, carry):
        other = lax.rem(me + k, sectors)
        pltpu.make_async_remote_copy(
            src_ref=fsend.at[other], dst_ref=frecv.at[me], send_sem=f_send.at[other], recv_sem=f_recv.at[me],
            device_id=(band, other), device_id_type=MESH,
        ).start()
        return carry

    lax.fori_loop(1, sectors, back_start, 0)
    frecv[me] = fsend[me]

    def back_wait(k, carry):
        other = lax.rem(me + k, sectors)
        pltpu.make_async_remote_copy(
            src_ref=fsend.at[me], dst_ref=frecv.at[other], send_sem=f_send.at[other], recv_sem=f_recv.at[other],
            device_id=(band, other), device_id_type=MESH,
        ).wait_recv()
        return carry

    lax.fori_loop(1, sectors, back_wait, 0)

    units = 2 * rows
    to_north = pltpu.make_async_remote_copy(
        src_ref=frecv.at[units - 1], dst_ref=frecv.at[units], send_sem=v_send.at[0], recv_sem=v_recv.at[0],
        device_id=(north, me), device_id_type=MESH,
    )
    to_south = pltpu.make_async_remote_copy(
        src_ref=frecv.at[1], dst_ref=frecv.at[units + 1], send_sem=v_send.at[1], recv_sem=v_recv.at[1],
        device_id=(south, me), device_id_type=MESH,
    )
    to_north.start()
    to_south.start()
    to_north.wait()
    to_south.wait()

    zero = jnp.zeros((8, 128), jnp.float32)
    merid = [frecv[units]] + [frecv[2 * r + 1] for r in range(rows)] + [frecv[units + 1]]
    merid = [pltpu.roll(m, 127, 1) for m in merid]
    faces = [0.5 * (merid[r] + merid[r + 1]) for r in range(rows + 1)]
    faces[0] = jnp.where(band == 0, 0.0, faces[0])
    faces[rows] = jnp.where(band == bands - 1, 0.0, faces[rows])
    ahead = [jnp.maximum(f, 0.0) for f in faces]
    back = [jnp.minimum(f, 0.0) for f in faces]
    for r in range(rows):
        u = frecv[2 * r]
        face = 0.5 * (u + pltpu.roll(u, 127, 1))
        west_p, west_m = jnp.maximum(face, 0.0), jnp.minimum(face, 0.0)
        face = pltpu.roll(face, 127, 1)
        east_p, east_m = jnp.maximum(face, 0.0), jnp.minimum(face, 0.0)
        centre = 1.0 - (east_p - west_m) - (ahead[r + 1] - back[r])
        for n, (a, b) in enumerate(((centre, -east_m), (west_p, -back[r + 1]), (ahead[r], zero))):
            at = 16 * (r % 8)
            turn[n, r // 8, at : at + 8, :] = jnp.where(low, a, pltpu.roll(b, 64, 1))
            turn[n, r // 8, at + 8 : at + 16, :] = jnp.where(low, pltpu.roll(a, 64, 1), b)
    for n in range(3):
        for octet in range(octets):
            coefs[n, octet] = turn[n, octet].T

    load.wait()
    for copy in edges:
        copy.wait()

    own = lax.div(lane, LEV) == sub

    def expand(n, octet, place):
        x = coefs[n, octet, pl.ds(place, 8, stride=0), :]
        x = jnp.where(own, x, 0.0)
        for turnby in (64, 32, 16):
            x = x + pltpu.roll(x, turnby, 1)
        return x

    modes_width = width // MOMENTS

    def column(j, carry):
        places = [(0, j), (0, 64 + j), (1, j), (1, 64 + j), (2, j)]
        stencil = [[expand(n, octet, place) for n, place in places] for octet in range(octets)]
        for part in range(modes_width // 128):
            advected = [[] for _ in range(octets)]
            for k in range(MOMENTS):
                lanes = pl.ds(k * modes_width + part * 128, 128)
                q = [tbuf[j + 1, 8 * o : 8 * o + 8, lanes] for o in range(octets)]
                north_row = jnp.broadcast_to(north_buf[j, :, lanes], (8, 128))
                south_row = jnp.broadcast_to(south_buf[j, :, lanes], (8, 128))
                down = [pltpu.roll(a, 7, 0) for a in q] + [north_row]
                up = [south_row] + [pltpu.roll(a, 1, 0) for a in q]
                for o in range(octets):
                    c, ce, cw, cn, cs = stencil[o]
                    above = jnp.where(sub < 7, down[o], down[o + 1])
                    below = jnp.where(sub > 0, up[o + 1], up[o])
                    octet_rows = pl.ds(8 * o, 8)
                    value = c * q[o] + ce * tbuf[j + 2, octet_rows, lanes] + cw * tbuf[j, octet_rows, lanes]
                    advected[o].append(value + cn * above + cs * below)
            for o in range(octets):
                updated = moment_sources(advected[o], rates[0, part], rates[1, part])
                for k in range(MOMENTS):
                    obuf[j, 8 * o : 8 * o + 8, pl.ds(k * modes_width + part * 128, 128)] = updated[k]
        pltpu.make_async_copy(obuf.at[j], out_ref.at[j], store_sem.at[j]).start()
        return carry

    lax.fori_loop(0, cols, column, 0)

    def store_wait(j, carry):
        pltpu.make_async_copy(obuf.at[j], out_ref.at[j], store_sem.at[j]).wait()
        return carry

    lax.fori_loop(0, cols, store_wait, 0)

    def send_wait(k, carry):
        other = lax.rem(me + k, sectors)
        wind_copy(k).wait_send()
        pltpu.make_async_remote_copy(
            src_ref=fsend.at[other], dst_ref=frecv.at[me], send_sem=f_send.at[other], recv_sem=f_recv.at[me],
            device_id=(band, other), device_id_type=MESH,
        ).wait_send()
        return carry

    lax.fori_loop(1, sectors, send_wait, 0)


def local(bands, sectors, tracers, winds, row_mask, coag_rate, growth_rate):
    rows, cols, width = tracers.shape
    lines = jnp.asarray(filter_lines(sectors, cols))
    f32, bf16 = jnp.float32, jnp.bfloat16
    dma = pltpu.SemaphoreType.DMA
    anywhere = pl.BlockSpec(memory_space=pl.ANY)
    scalars = pl.BlockSpec(memory_space=pltpu.SMEM)
    out = pl.pallas_call(
        functools.partial(kernel, bands, sectors),
        out_shape=jax.ShapeDtypeStruct((cols, rows, width), f32),
        in_specs=[anywhere, scalars, scalars, scalars, pl.BlockSpec(memory_space=pltpu.VMEM), anywhere],
        out_specs=anywhere,
        scratch_shapes=[
            pltpu.VMEM((sectors, 128), f32),
            pltpu.VMEM((sectors, 8, 128), f32),
            pltpu.VMEM((sectors, 8, 128), f32),
            pltpu.VMEM((sectors, 8, 128), f32),
            pltpu.VMEM((sectors + 2, 8, 128), f32),
            pltpu.VMEM((8 * sectors, 64 * sectors), bf16),
            pltpu.VMEM((8 * sectors, 64 * sectors), bf16),
            pltpu.VMEM((64 * sectors, 128), bf16),
            pltpu.VMEM((64 * sectors, 128), bf16),
            pltpu.VMEM((3, rows // 8, 128, 128), f32),
            pltpu.VMEM((3, rows // 8, 128, 128), f32),
            pltpu.VMEM((2, 2, 8, 128), f32),
            pltpu.VMEM((cols + 2, rows, width), f32),
            pltpu.VMEM((cols, rows, width), f32),
            pltpu.VMEM((cols, 1, width), f32),
            pltpu.VMEM((cols, 1, width), f32),
            dma, dma, dma((cols,)),
            dma((sectors,)), dma((sectors,)), dma((sectors,)), dma((sectors,)),
            dma((4,)), dma((4,)), dma((2,)), dma((2,)),
        ],
        compiler_params=pltpu.CompilerParams(collective_id=0, has_side_effects=True),
        name="transport",
    )(lines, row_mask, coag_rate, growth_rate, jnp.transpose(winds, (0, 2, 1)), jnp.transpose(tracers, (1, 0, 2)))
    return jnp.transpose(out, (1, 0, 2))


def solution(mesh):
    bands, sectors = mesh.shape["lat"], mesh.shape["lon"]
    return jax.shard_map(
        functools.partial(local, bands, sectors),
        mesh=mesh,
        in_specs=(P("lat", "lon", None), P("lat", "lon", None), P("lat"), P(), P()),
        out_specs=P("lat", "lon", None),
        check_vma=False,
    )
```

```python
import functools
import math

import jax
import jax.numpy as jnp
import numpy as np
from jax import lax
from jax.experimental import pallas as pl
from jax.experimental.pallas import tpu as pltpu
from jax.sharding import PartitionSpec as P

NLON = 1440
GLOBE_ROWS = 720
LEV = 16
MODES = 16
MOMENTS = 6
FILTER_ROWS = 48
GROUPS = 5
MESH = pl.DeviceIdType.MESH

POLY = (
    0.5000000260258313,
    0.577346917369578,
    -0.11103851124670026,
    0.052841409139758516,
    -0.03023539756350864,
    0.016047280362516254,
    -0.0060893456734267045,
    0.0011276362373084019,
)


def filter_lines(sectors, cols):
    rows = np.arange(FILTER_ROWS)
    angles = (-90.0 + 180.0 * (rows + 0.5) / GLOBE_ROWS) * (math.pi / 180.0)
    cosines = np.cos(angles)[:, None]
    sines = np.sin(np.arange(NLON // 2 + 1) * (math.pi / NLON))[None, :]
    factor = cosines / np.maximum(math.cos(math.pi / 4.0) * sines, cosines)
    kernel = np.fft.irfft(factor, n=NLON, axis=1)
    lane = np.arange(128)
    shift = np.where(lane < 64, lane, lane - 128)
    place = (cols * np.arange(sectors)[:, None] - 1 + shift[None, :]) % NLON
    return kernel[:, place].astype(np.float32)


def split_two(x):
    high = x.astype(jnp.bfloat16)
    return high, (x - high.astype(jnp.float32)).astype(jnp.bfloat16)


def positive_root(x):
    return x * lax.rsqrt(x)


def moment_sources(moments, coag, growth):
    m0, m1, m2, m3, m4, m5 = moments
    inv0 = 1.0 / m0
    a0 = m1 * inv0
    s1 = m2 - a0 * m1
    s2 = m3 - a0 * m2
    s3 = m4 - a0 * m3
    s4 = m5 - a0 * m4
    inv1 = 1.0 / s1
    r21 = s2 * inv1
    a1 = r21 - a0
    b1 = s1 * inv0
    t2 = s3 - a1 * s2 - b1 * m2
    t3 = s4 - a1 * s3 - b1 * m3
    a2 = t3 * (1.0 / t2) - r21
    b2 = t2 * inv1
    d1, d2 = a1 - a0, a2 - a0
    c = (d1 + d2) * (1.0 / 3.0)
    e2 = d1 * d2 - (b1 + b2)
    cc = c * c
    p2 = cc - (1.0 / 3.0) * e2
    inv_p = lax.rsqrt(p2)
    p = p2 * inv_p
    half_h = c * (0.5 * cc - 0.25 * e2) - 0.25 * (b1 * d2)
    half_h = half_h * (inv_p * (inv_p * inv_p))
    u = positive_root(jnp.clip(0.5 + half_h, 1e-30, 1.0))
    cosine = POLY[-1] * u + POLY[-2]
    for coef in POLY[-3::-1]:
        cosine = cosine * u + coef
    sine = positive_root(jnp.maximum(1.0 - cosine * cosine, 1e-30))
    along, across = p * cosine, (math.sqrt(3.0) * p) * sine
    rest = c - along
    ys = (c + (along + along), rest + across, rest - across)
    xs = [y + a0 for y in ys]
    gaps = (ys[0] - ys[1], ys[0] - ys[2], ys[1] - ys[2])
    dens = (gaps[0] * gaps[1], -gaps[0] * gaps[2], gaps[1] * gaps[2])
    ws, shares = [], []
    for i, j, k in ((0, 1, 2), (1, 0, 2), (2, 0, 1)):
        above = 1.0 + xs[i]
        share = (s1 + m0 * (ys[j] * ys[k])) / (dens[i] * above)
        ws.append(share * above)
        shares.append(share)
    vs = [x * x * x for x in xs]
    cw = [w * coag for w in ws]
    wv = [ws[i] * vs[i] for i in range(3)]
    diag = [cw[i] * wv[i] for i in range(3)]
    q7 = [wv[i] * (vs[i] * xs[i]) for i in range(3)]
    q8 = [q7[i] * xs[i] for i in range(3)]
    higher = (m3, m4, m5, None, q7[0] + q7[1] + q7[2], q8[0] + q8[1] + q8[2])
    pairs, roots, joins = [], [], []
    for i, j in ((0, 1), (0, 2), (1, 2)):
        joined = vs[i] + vs[j]
        roots.append(jnp.exp2(jnp.log(joined) * (math.log2(math.e) / 3.0)))
        pairs.append(cw[i] * ws[j] * joined)
        joins.append(joined)
    cm0, cm3 = coag * m0, coag * m3
    out = [m0 - cm0 * m3]
    grown = shares[0] + shares[1] + shares[2]
    first = pairs
    for k in range(1, MOMENTS):
        pairs = [pairs[i] * roots[i] for i in range(3)]
        diag = [diag[i] * xs[i] for i in range(3)]
        total = moments[k] + (float(k) * growth) * grown
        grown = moments[k - 1] - grown
        if k == 3:
            left = [pairs[i] - first[i] * joins[i] for i in range(3)]
            total = total + (left[0] + left[1] + left[2])
        else:
            total = total + (pairs[0] + pairs[1] + pairs[2]) - (cm0 * higher[k] + cm3 * moments[k])
            total = total + 2.0 ** (k / 3.0) * (diag[0] + diag[1] + diag[2])
        out.append(total)
    return out


def kernel(
    bands, sectors, lines_ref, mask_ref, coag_ref, growth_ref, winds_ref, tracers_ref, out_ref,
    line_buf, wsend, wrecv, fsend, frecv, wide, table_h, table_l, turn, coefs, rates,
    tbuf, south_buf, north_buf,
    line_sem, load_sem, w_send, w_recv, f_send, f_recv, edge_send, edge_recv, row_send, row_recv, v_send,
):
    band, me = lax.axis_index("lat"), lax.axis_index("lon")
    north, south = lax.rem(band + 1, bands), lax.rem(band + bands - 1, bands)
    east, west = lax.rem(me + 1, sectors), lax.rem(me + sectors - 1, sectors)
    rows, channels, cols = winds_ref.shape
    width = tracers_ref.shape[-1]
    octets = rows // 8
    lane = lax.broadcasted_iota(jnp.int32, (8, 128), 1)
    sub = lax.broadcasted_iota(jnp.int32, (8, 128), 0)
    low = lane < 64

    barrier = pltpu.get_barrier_semaphore()

    def greet(k, carry):
        pl.semaphore_signal(barrier, inc=1, device_id=(band, lax.rem(me + k, sectors)), device_id_type=MESH)
        return carry

    lax.fori_loop(1, sectors, greet, 0)
    for other in (north, south):
        pl.semaphore_signal(barrier, inc=1, device_id=(other, me), device_id_type=MESH)
    pl.semaphore_signal(barrier, inc=1, device_id=(north, 1), device_id_type=MESH)
    pl.semaphore_signal(barrier, inc=1, device_id=(south, sectors - 1), device_id_type=MESH)

    unit_row = lax.div(me, 2)
    line = jnp.minimum(band * rows + unit_row, FILTER_ROWS - 1)
    line_copy = pltpu.make_async_copy(lines_ref.at[line], line_buf, line_sem)
    line_copy.start()
    load = pltpu.make_async_copy(tracers_ref, tbuf.at[pl.ds(1, cols)], load_sem)
    load.start()

    for unit in range(2 * rows):
        wsend[unit] = jnp.zeros((8, 128), jnp.float32)
        for g in range(2):
            start = 16 * (unit % 2) + 8 * g
            wsend[unit, :, 64 * g : 64 * g + cols] = winds_ref[unit // 2, start : start + 8, :]
    for half in range(2):
        c = jnp.zeros((8, 128), jnp.float32)
        g = jnp.zeros((8, 128), jnp.float32)
        for mode in range(8):
            here = lax.div(lane, LEV) == mode
            c = jnp.where(here, coag_ref[8 * half + mode], c)
            g = jnp.where(here, growth_ref[8 * half + mode], g)
        rates[0, half] = c
        rates[1, half] = g

    line_copy.wait()
    filtered = mask_ref[unit_row] > 0
    for k in range(sectors):
        parts = []
        for side in range(2):
            e = (side - k) % sectors
            values = line_buf[e : e + 1, :]
            unit_line = jnp.zeros((1, 128), jnp.float32)
            for x in range(128):
                if (cols * e - 1 + (x if x < 64 else x - 128)) % NLON == 0:
                    unit_line = jnp.where(lax.broadcasted_iota(jnp.int32, (1, 128), 1) == x, 1.0, unit_line)
            values = jnp.where(filtered, values, unit_line)
            parts.append(pltpu.roll(jnp.broadcast_to(values, (64, 128)), 64 * side, 1, stride=1, stride_axis=0))
        left = lax.broadcasted_iota(jnp.int32, (64, 128), 1) < 64
        high, rest = split_two(jnp.where(left, parts[0], parts[1]))
        for at, lanes in ((64 * k, 0), (64 * ((k + 2) % sectors), 128)):
            table_h[at : at + 64, lanes : lanes + 128] = high
            table_l[at : at + 64, lanes : lanes + 128] = rest

    extra = jnp.where(jnp.logical_or(me == 1, me == sectors - 1), sectors, 0)
    pl.semaphore_wait(barrier, sectors + 1 + extra)

    def wind_copy(k):
        other = lax.rem(me + k, sectors)
        return pltpu.make_async_remote_copy(
            src_ref=wsend.at[other], dst_ref=wrecv.at[me], send_sem=w_send.at[other], recv_sem=w_recv.at[me],
            device_id=(band, other), device_id_type=MESH,
        )

    def wind_start(k, carry):
        wind_copy(k).start()
        return carry

    lax.fori_loop(1, sectors, wind_start, 0)
    wrecv[me] = wsend[me]

    edges = [
        pltpu.make_async_remote_copy(
            src_ref=tracers_ref.at[cols - 1], dst_ref=tbuf.at[0], send_sem=edge_send.at[0], recv_sem=edge_recv.at[0],
            device_id=(band, east), device_id_type=MESH,
        ),
        pltpu.make_async_remote_copy(
            src_ref=tracers_ref.at[0], dst_ref=tbuf.at[cols + 1], send_sem=edge_send.at[1], recv_sem=edge_recv.at[1],
            device_id=(band, west), device_id_type=MESH,
        ),
    ]
    for copy in edges:
        copy.start()

    groups = GROUPS
    size = cols // groups

    def row_copies(g):
        here = pl.ds(g * size, size)
        return [
            pltpu.make_async_remote_copy(
                src_ref=tracers_ref.at[here, pl.ds(row, 1), :], dst_ref=dst.at[here], send_sem=row_send.at[side, g],
                recv_sem=row_recv.at[side, g], device_id=(target, me), device_id_type=MESH,
            )
            for side, (row, dst, target) in enumerate(((rows - 1, south_buf, north), (0, north_buf, south)))
        ]

    @pl.loop(0, groups)
    def _(g):
        for copy in row_copies(g):
            copy.start()

    def wind_wait(k, carry):
        other = lax.rem(me + k, sectors)
        pltpu.make_async_remote_copy(
            src_ref=wsend.at[me], dst_ref=wrecv.at[other], send_sem=w_send.at[other], recv_sem=w_recv.at[other],
            device_id=(band, other), device_id_type=MESH,
        ).wait_recv()
        return carry

    lax.fori_loop(1, sectors, wind_wait, 0)

    pairs, quads = sectors // 2, sectors // 4
    for q in range(pairs):
        one, two = wrecv[2 * q], wrecv[2 * q + 1]
        block = jnp.concatenate(
            [jnp.where(low, one, pltpu.roll(two, 64, 1)), jnp.where(low, pltpu.roll(one, 64, 1), two)], axis=0
        )
        high, rest = split_two(block)
        for p in range(quads):
            at = 128 * ((q - 2 * p) % pairs)
            wide[16 * p : 16 * p + 16, at : at + 128] = high
            wide[16 * (quads + p) : 16 * (quads + p) + 16, at : at + 128] = rest
    both = jnp.dot(wide[...], table_h[...], preferred_element_type=jnp.float32)
    rest = jnp.dot(wide[0 : 16 * quads, :], table_l[...], preferred_element_type=jnp.float32)
    smooth = both[0 : 16 * quads] + (both[16 * quads :] + rest)
    for p in range(pairs):
        at, lanes = 16 * (p // 2), 128 * (p % 2)
        one, two = smooth[at : at + 8, lanes : lanes + 128], smooth[at + 8 : at + 16, lanes : lanes + 128]
        fsend[2 * p] = jnp.where(low, one, pltpu.roll(two, 64, 1))
        fsend[2 * p + 1] = jnp.where(low, pltpu.roll(one, 64, 1), two)

    units = 2 * rows
    last_unit = units - 1

    def back_copy(k):
        other = lax.rem(me + k, sectors)
        return pltpu.make_async_remote_copy(
            src_ref=fsend.at[other], dst_ref=frecv.at[me], send_sem=f_send.at[other], recv_sem=f_recv.at[me],
            device_id=(band, other), device_id_type=MESH,
        )

    def beyond_copy(k, slot, target):
        other = lax.rem(me + k, sectors)
        return pltpu.make_async_remote_copy(
            src_ref=fsend.at[other], dst_ref=frecv.at[slot], send_sem=v_send.at[other], recv_sem=f_recv.at[slot],
            device_id=(target, other), device_id_type=MESH,
        )

    def each(start, body):
        def step(k, carry):
            body(k)
            return carry

        lax.fori_loop(start, sectors, step, 0)

    @pl.when(me == last_unit)
    def _():
        each(0, lambda k: beyond_copy(k, units, north).start())

    @pl.when(me == 1)
    def _():
        each(0, lambda k: beyond_copy(k, units + 1, south).start())

    each(1, lambda k: back_copy(k).start())
    frecv[me] = fsend[me]

    def arrived(slot):
        pltpu.make_async_remote_copy(
            src_ref=fsend.at[me], dst_ref=frecv.at[slot], send_sem=f_send.at[me], recv_sem=f_recv.at[slot],
            device_id=(band, east), device_id_type=MESH,
        ).wait_recv()

    each(1, lambda k: arrived(lax.rem(me + k, sectors)))
    arrived(units)
    arrived(units + 1)

    zero = jnp.zeros((8, 128), jnp.float32)
    merid = [frecv[units]] + [frecv[2 * r + 1] for r in range(rows)] + [frecv[units + 1]]
    merid = [pltpu.roll(m, 127, 1) for m in merid]
    faces = [0.5 * (merid[r] + merid[r + 1]) for r in range(rows + 1)]
    faces[0] = jnp.where(band == 0, 0.0, faces[0])
    faces[rows] = jnp.where(band == bands - 1, 0.0, faces[rows])
    ahead = [jnp.maximum(f, 0.0) for f in faces]
    back = [jnp.minimum(f, 0.0) for f in faces]
    for r in range(rows):
        u = frecv[2 * r]
        face = 0.5 * (u + pltpu.roll(u, 127, 1))
        west_p, west_m = jnp.maximum(face, 0.0), jnp.minimum(face, 0.0)
        face = pltpu.roll(face, 127, 1)
        east_p, east_m = jnp.maximum(face, 0.0), jnp.minimum(face, 0.0)
        centre = 1.0 - (east_p - west_m) - (ahead[r + 1] - back[r])
        for n, (a, b) in enumerate(((centre, -east_m), (west_p, -back[r + 1]), (ahead[r], zero))):
            at = 16 * (r % 8)
            turn[n, r // 8, at : at + 8, :] = jnp.where(low, a, pltpu.roll(b, 64, 1))
            turn[n, r // 8, at + 8 : at + 16, :] = jnp.where(low, pltpu.roll(a, 64, 1), b)
    for n in range(3):
        for octet in range(octets):
            coefs[n, octet] = turn[n, octet].T

    load.wait()
    for copy in edges:
        copy.wait_recv()

    own = lax.div(lane, LEV) == sub

    def expand(n, octet, place):
        x = coefs[n, octet, pl.ds(place, 8, stride=0), :]
        x = jnp.where(own, x, 0.0)
        for turnby in (64, 32, 16):
            x = x + pltpu.roll(x, turnby, 1)
        return x

    modes_width = width // MOMENTS

    def column(j, carry):
        places = [(0, j), (0, 64 + j), (1, j), (1, 64 + j), (2, j)]
        stencil = [[expand(n, octet, place) for n, place in places] for octet in range(octets)]
        for part in range(modes_width // 128):
            advected = [[] for _ in range(octets)]
            for k in range(MOMENTS):
                lanes = pl.ds(k * modes_width + part * 128, 128)
                q = [tbuf[j + 1, 8 * o : 8 * o + 8, lanes] for o in range(octets)]
                north_row = jnp.broadcast_to(north_buf[j, :, lanes], (8, 128))
                south_row = jnp.broadcast_to(south_buf[j, :, lanes], (8, 128))
                down = [pltpu.roll(a, 7, 0) for a in q] + [north_row]
                up = [south_row] + [pltpu.roll(a, 1, 0) for a in q]
                for o in range(octets):
                    c, ce, cw, cn, cs = stencil[o]
                    above = jnp.where(sub < 7, down[o], down[o + 1])
                    below = jnp.where(sub > 0, up[o + 1], up[o])
                    octet_rows = pl.ds(8 * o, 8)
                    value = c * q[o] + ce * tbuf[j + 2, octet_rows, lanes] + cw * tbuf[j, octet_rows, lanes]
                    advected[o].append(value + cn * above + cs * below)
            for o in range(octets):
                updated = moment_sources(advected[o], rates[0, part], rates[1, part])
                for k in range(MOMENTS):
                    out_ref[j, 8 * o : 8 * o + 8, pl.ds(k * modes_width + part * 128, 128)] = updated[k]
        return carry

    @pl.loop(0, groups)
    def _(g):
        for copy in row_copies(g):
            copy.wait_recv()
        lax.fori_loop(g * size, g * size + size, column, 0)

    each(1, lambda k: wind_copy(k).wait_send())
    each(1, lambda k: back_copy(k).wait_send())

    @pl.when(me == last_unit)
    def _():
        each(0, lambda k: beyond_copy(k, units, north).wait_send())

    @pl.when(me == 1)
    def _():
        each(0, lambda k: beyond_copy(k, units + 1, south).wait_send())

    for copy in edges:
        copy.wait_send()

    @pl.loop(0, groups)
    def _(g):
        for copy in row_copies(g):
            copy.wait_send()


def local(bands, sectors, tracers, winds, row_mask, coag_rate, growth_rate):
    rows, cols, width = tracers.shape
    lines = jnp.asarray(filter_lines(sectors, cols))
    f32, bf16 = jnp.float32, jnp.bfloat16
    dma = pltpu.SemaphoreType.DMA
    anywhere = pl.BlockSpec(memory_space=pltpu.HBM)
    scalars = pl.BlockSpec(memory_space=pltpu.SMEM)
    out = pl.pallas_call(
        functools.partial(kernel, bands, sectors),
        out_shape=pltpu.VMEM((cols, rows, width), f32),
        in_specs=[anywhere, scalars, scalars, scalars, pl.BlockSpec(memory_space=pltpu.VMEM), anywhere],
        out_specs=pl.BlockSpec(memory_space=pltpu.VMEM),
        scratch_shapes=[
            pltpu.VMEM((sectors, 128), f32),
            pltpu.VMEM((sectors, 8, 128), f32),
            pltpu.VMEM((sectors, 8, 128), f32),
            pltpu.VMEM((sectors, 8, 128), f32),
            pltpu.VMEM((sectors + 2, 8, 128), f32),
            pltpu.VMEM((8 * sectors, 64 * sectors), bf16),
            pltpu.VMEM((64 * sectors, 256), bf16),
            pltpu.VMEM((64 * sectors, 256), bf16),
            pltpu.VMEM((3, rows // 8, 128, 128), f32),
            pltpu.VMEM((3, rows // 8, 128, 128), f32),
            pltpu.VMEM((2, 2, 8, 128), f32),
            pltpu.VMEM((cols + 2, rows, width), f32),
            pltpu.VMEM((cols, 1, width), f32),
            pltpu.VMEM((cols, 1, width), f32),
            dma, dma,
            dma((sectors,)), dma((sectors,)), dma((sectors,)), dma((sectors + 2,)),
            dma((2,)), dma((2,)), dma((2, GROUPS)), dma((2, GROUPS)), dma((sectors,)),
        ],
        compiler_params=pltpu.CompilerParams(collective_id=0, has_side_effects=True, vmem_limit_bytes=67043328 - 4 * cols * rows * width),
        name="transport",
    )(lines, row_mask, coag_rate, growth_rate, jnp.transpose(winds, (0, 2, 1)), jnp.transpose(tracers, (1, 0, 2)))
    return jnp.transpose(out, (1, 0, 2))


def solution(mesh):
    bands, sectors = mesh.shape["lat"], mesh.shape["lon"]
    return jax.shard_map(
        functools.partial(local, bands, sectors),
        mesh=mesh,
        in_specs=(P("lat", "lon", None), P("lat", "lon", None), P("lat"), P(), P()),
        out_specs=P("lat", "lon", None),
        check_vma=False,
    )
```

```python
import functools
import math

import jax
import jax.numpy as jnp
import numpy as np
from jax import lax
from jax.experimental import pallas as pl
from jax.experimental.pallas import tpu as pltpu
from jax.sharding import PartitionSpec as P

NLON = 1440
GLOBE_ROWS = 720
LEV = 16
MODES = 16
MOMENTS = 6
FILTER_ROWS = 48
GROUP = 4
MESH = pl.DeviceIdType.MESH

POLY = (
    0.5000000260258313,
    0.577346917369578,
    -0.11103851124670026,
    0.052841409139758516,
    -0.03023539756350864,
    0.016047280362516254,
    -0.0060893456734267045,
    0.0011276362373084019,
)


def filter_lines(sectors, cols):
    rows = np.arange(FILTER_ROWS)
    angles = (-90.0 + 180.0 * (rows + 0.5) / GLOBE_ROWS) * (math.pi / 180.0)
    cosines = np.cos(angles)[:, None]
    sines = np.sin(np.arange(NLON // 2 + 1) * (math.pi / NLON))[None, :]
    factor = cosines / np.maximum(math.cos(math.pi / 4.0) * sines, cosines)
    kernel = np.fft.irfft(factor, n=NLON, axis=1)
    lane = np.arange(128)
    shift = np.where(lane < 64, lane, lane - 128)
    place = (cols * np.arange(sectors)[:, None] - 1 + shift[None, :]) % NLON
    return kernel[:, place].astype(np.float32)


def split_two(x):
    high = x.astype(jnp.bfloat16)
    return high, (x - high.astype(jnp.float32)).astype(jnp.bfloat16)


def positive_root(x):
    return x * lax.rsqrt(x)


def moment_sources(moments, coag, growth):
    m0, m1, m2, m3, m4, m5 = moments
    inv0 = 1.0 / m0
    a0 = m1 * inv0
    s1 = m2 - a0 * m1
    s2 = m3 - a0 * m2
    s3 = m4 - a0 * m3
    s4 = m5 - a0 * m4
    inv1 = 1.0 / s1
    r21 = s2 * inv1
    a1 = r21 - a0
    b1 = s1 * inv0
    t2 = s3 - a1 * s2 - b1 * m2
    t3 = s4 - a1 * s3 - b1 * m3
    a2 = t3 * (1.0 / t2) - r21
    b2 = t2 * inv1
    d1, d2 = a1 - a0, a2 - a0
    c = (d1 + d2) * (1.0 / 3.0)
    e2 = d1 * d2 - (b1 + b2)
    cc = c * c
    p2 = cc - (1.0 / 3.0) * e2
    inv_p = lax.rsqrt(p2)
    p = p2 * inv_p
    half_h = c * (0.5 * cc - 0.25 * e2) - 0.25 * (b1 * d2)
    half_h = half_h * (inv_p * (inv_p * inv_p))
    u = positive_root(jnp.clip(0.5 + half_h, 1e-30, 1.0))
    cosine = POLY[-1] * u + POLY[-2]
    for coef in POLY[-3::-1]:
        cosine = cosine * u + coef
    sine = positive_root(jnp.maximum(1.0 - cosine * cosine, 1e-30))
    along, across = p * cosine, (math.sqrt(3.0) * p) * sine
    rest = c - along
    ys = (c + (along + along), rest + across, rest - across)
    xs = [y + a0 for y in ys]
    gaps = (ys[0] - ys[1], ys[0] - ys[2], ys[1] - ys[2])
    dens = (gaps[0] * gaps[1], -gaps[0] * gaps[2], gaps[1] * gaps[2])
    ws, shares = [], []
    for i, j, k in ((0, 1, 2), (1, 0, 2), (2, 0, 1)):
        above = 1.0 + xs[i]
        share = (s1 + m0 * (ys[j] * ys[k])) / (dens[i] * above)
        ws.append(share * above)
        shares.append(share)
    vs = [x * x * x for x in xs]
    cw = [w * coag for w in ws]
    wv = [ws[i] * vs[i] for i in range(3)]
    diag = [cw[i] * wv[i] for i in range(3)]
    q7 = [wv[i] * (vs[i] * xs[i]) for i in range(3)]
    q8 = [q7[i] * xs[i] for i in range(3)]
    higher = (m3, m4, m5, None, q7[0] + q7[1] + q7[2], q8[0] + q8[1] + q8[2])
    pairs, roots, joins = [], [], []
    for i, j in ((0, 1), (0, 2), (1, 2)):
        joined = vs[i] + vs[j]
        roots.append(jnp.exp2(jnp.log(joined) * (math.log2(math.e) / 3.0)))
        pairs.append(cw[i] * ws[j] * joined)
        joins.append(joined)
    cm0, cm3 = coag * m0, coag * m3
    out = [m0 - cm0 * m3]
    grown = shares[0] + shares[1] + shares[2]
    first = pairs
    for k in range(1, MOMENTS):
        pairs = [pairs[i] * roots[i] for i in range(3)]
        diag = [diag[i] * xs[i] for i in range(3)]
        total = moments[k] + (float(k) * growth) * grown
        grown = moments[k - 1] - grown
        if k == 3:
            left = [pairs[i] - first[i] * joins[i] for i in range(3)]
            total = total + (left[0] + left[1] + left[2])
        else:
            total = total + (pairs[0] + pairs[1] + pairs[2]) - (cm0 * higher[k] + cm3 * moments[k])
            total = total + 2.0 ** (k / 3.0) * (diag[0] + diag[1] + diag[2])
        out.append(total)
    return out


def kernel(
    bands, sectors, lines_ref, mask_ref, coag_ref, growth_ref, winds_ref, tracers_ref, out_ref,
    line_buf, wsend, wrecv, fsend, frecv, wide, table_h, table_l, turn, coefs, rates,
    tbuf, south_buf, north_buf, even, odd,
    line_sem, load_sem, w_send, w_recv, f_send, f_recv, edge_send, edge_recv, row_send, row_recv, v_send,
):
    band, me = lax.axis_index("lat"), lax.axis_index("lon")
    north, south = lax.rem(band + 1, bands), lax.rem(band + bands - 1, bands)
    east, west = lax.rem(me + 1, sectors), lax.rem(me + sectors - 1, sectors)
    rows, channels, cols = winds_ref.shape
    width = tracers_ref.shape[-1]
    octets = rows // 8
    lane = lax.broadcasted_iota(jnp.int32, (8, 128), 1)
    sub = lax.broadcasted_iota(jnp.int32, (8, 128), 0)
    low = lane < 64

    barrier = pltpu.get_barrier_semaphore()

    def greet(k, carry):
        pl.semaphore_signal(barrier, inc=1, device_id=(band, lax.rem(me + k, sectors)), device_id_type=MESH)
        return carry

    lax.fori_loop(1, sectors, greet, 0)
    for other in (north, south):
        pl.semaphore_signal(barrier, inc=1, device_id=(other, me), device_id_type=MESH)
    pl.semaphore_signal(barrier, inc=1, device_id=(north, 1), device_id_type=MESH)
    pl.semaphore_signal(barrier, inc=1, device_id=(south, sectors - 1), device_id_type=MESH)

    unit_row = lax.div(me, 2)
    line = jnp.minimum(band * rows + unit_row, FILTER_ROWS - 1)
    line_copy = pltpu.make_async_copy(lines_ref.at[line], line_buf, line_sem)
    line_copy.start()
    load = pltpu.make_async_copy(tracers_ref, tbuf.at[pl.ds(1, cols)], load_sem)
    load.start()

    for unit in range(2 * rows):
        wsend[unit] = jnp.zeros((8, 128), jnp.float32)
        for g in range(2):
            start = 16 * (unit % 2) + 8 * g
            wsend[unit, :, 64 * g : 64 * g + cols] = winds_ref[unit // 2, start : start + 8, :]
    for half in range(2):
        c = jnp.zeros((8, 128), jnp.float32)
        g = jnp.zeros((8, 128), jnp.float32)
        for mode in range(8):
            here = lax.div(lane, LEV) == mode
            c = jnp.where(here, coag_ref[8 * half + mode], c)
            g = jnp.where(here, growth_ref[8 * half + mode], g)
        rates[0, half] = c
        rates[1, half] = g

    line_copy.wait()
    filtered = mask_ref[unit_row] > 0
    for k in range(sectors):
        parts = []
        for side in range(2):
            e = (side - k) % sectors
            values = line_buf[e : e + 1, :]
            unit_line = jnp.zeros((1, 128), jnp.float32)
            for x in range(128):
                if (cols * e - 1 + (x if x < 64 else x - 128)) % NLON == 0:
                    unit_line = jnp.where(lax.broadcasted_iota(jnp.int32, (1, 128), 1) == x, 1.0, unit_line)
            values = jnp.where(filtered, values, unit_line)
            parts.append(pltpu.roll(jnp.broadcast_to(values, (64, 128)), 64 * side, 1, stride=1, stride_axis=0))
        left = lax.broadcasted_iota(jnp.int32, (64, 128), 1) < 64
        high, rest = split_two(jnp.where(left, parts[0], parts[1]))
        for at, lanes in ((64 * k, 0), (64 * ((k + 2) % sectors), 128)):
            table_h[at : at + 64, lanes : lanes + 128] = high
            table_l[at : at + 64, lanes : lanes + 128] = rest

    extra = jnp.where(jnp.logical_or(me == 1, me == sectors - 1), sectors, 0)
    pl.semaphore_wait(barrier, sectors + 1 + extra)

    def wind_copy(k):
        other = lax.rem(me + k, sectors)
        return pltpu.make_async_remote_copy(
            src_ref=wsend.at[other], dst_ref=wrecv.at[me], send_sem=w_send.at[other], recv_sem=w_recv.at[me],
            device_id=(band, other), device_id_type=MESH,
        )

    def wind_start(k, carry):
        wind_copy(k).start()
        return carry

    lax.fori_loop(1, sectors, wind_start, 0)
    wrecv[me] = wsend[me]

    edges = [
        pltpu.make_async_remote_copy(
            src_ref=tracers_ref.at[cols - 1], dst_ref=tbuf.at[0], send_sem=edge_send.at[0], recv_sem=edge_recv.at[0],
            device_id=(band, east), device_id_type=MESH,
        ),
        pltpu.make_async_remote_copy(
            src_ref=tracers_ref.at[0], dst_ref=tbuf.at[cols + 1], send_sem=edge_send.at[1], recv_sem=edge_recv.at[1],
            device_id=(band, west), device_id_type=MESH,
        ),
    ]
    for copy in edges:
        copy.start()

    groups = (cols - 1) // GROUP

    def row_copies(slot, start, size):
        here = pl.ds(start, size)
        return [
            pltpu.make_async_remote_copy(
                src_ref=tracers_ref.at[here, pl.ds(row, 1), :], dst_ref=dst.at[here], send_sem=row_send.at[side, slot],
                recv_sem=row_recv.at[side, slot], device_id=(target, me), device_id_type=MESH,
            )
            for side, (row, dst, target) in enumerate(((rows - 1, south_buf, north), (0, north_buf, south)))
        ]

    def group_copies(g):
        return row_copies(g, GROUP * g + 1, GROUP)

    for copy in row_copies(groups, 0, 1):
        copy.start()

    @pl.loop(0, groups)
    def _(g):
        for copy in group_copies(g):
            copy.start()

    def wind_wait(k, carry):
        other = lax.rem(me + k, sectors)
        pltpu.make_async_remote_copy(
            src_ref=wsend.at[me], dst_ref=wrecv.at[other], send_sem=w_send.at[other], recv_sem=w_recv.at[other],
            device_id=(band, other), device_id_type=MESH,
        ).wait_recv()
        return carry

    lax.fori_loop(1, sectors, wind_wait, 0)

    pairs, quads = sectors // 2, sectors // 4
    for q in range(pairs):
        one, two = wrecv[2 * q], wrecv[2 * q + 1]
        block = jnp.concatenate(
            [jnp.where(low, one, pltpu.roll(two, 64, 1)), jnp.where(low, pltpu.roll(one, 64, 1), two)], axis=0
        )
        high, rest = split_two(block)
        for p in range(quads):
            at = 128 * ((q - 2 * p) % pairs)
            wide[16 * p : 16 * p + 16, at : at + 128] = high
            wide[16 * (quads + p) : 16 * (quads + p) + 16, at : at + 128] = rest
    both = jnp.dot(wide[...], table_h[...], preferred_element_type=jnp.float32)
    rest = jnp.dot(wide[0 : 16 * quads, :], table_l[...], preferred_element_type=jnp.float32)
    smooth = both[0 : 16 * quads] + (both[16 * quads :] + rest)
    for p in range(pairs):
        at, lanes = 16 * (p // 2), 128 * (p % 2)
        one, two = smooth[at : at + 8, lanes : lanes + 128], smooth[at + 8 : at + 16, lanes : lanes + 128]
        fsend[2 * p] = jnp.where(low, one, pltpu.roll(two, 64, 1))
        fsend[2 * p + 1] = jnp.where(low, pltpu.roll(one, 64, 1), two)

    units = 2 * rows
    last_unit = units - 1

    def back_copy(k):
        other = lax.rem(me + k, sectors)
        return pltpu.make_async_remote_copy(
            src_ref=fsend.at[other], dst_ref=frecv.at[me], send_sem=f_send.at[other], recv_sem=f_recv.at[me],
            device_id=(band, other), device_id_type=MESH,
        )

    def beyond_copy(k, slot, target):
        other = lax.rem(me + k, sectors)
        return pltpu.make_async_remote_copy(
            src_ref=fsend.at[other], dst_ref=frecv.at[slot], send_sem=v_send.at[other], recv_sem=f_recv.at[slot],
            device_id=(target, other), device_id_type=MESH,
        )

    def each(start, body):
        def step(k, carry):
            body(k)
            return carry

        lax.fori_loop(start, sectors, step, 0)

    @pl.when(me == last_unit)
    def _():
        each(0, lambda k: beyond_copy(k, units, north).start())

    @pl.when(me == 1)
    def _():
        each(0, lambda k: beyond_copy(k, units + 1, south).start())

    each(1, lambda k: back_copy(k).start())
    frecv[me] = fsend[me]

    def arrived(slot):
        pltpu.make_async_remote_copy(
            src_ref=fsend.at[me], dst_ref=frecv.at[slot], send_sem=f_send.at[me], recv_sem=f_recv.at[slot],
            device_id=(band, east), device_id_type=MESH,
        ).wait_recv()

    each(1, lambda k: arrived(lax.rem(me + k, sectors)))
    arrived(units)
    arrived(units + 1)

    zero = jnp.zeros((8, 128), jnp.float32)
    merid = [frecv[units]] + [frecv[2 * r + 1] for r in range(rows)] + [frecv[units + 1]]
    merid = [pltpu.roll(m, 127, 1) for m in merid]
    faces = [0.5 * (merid[r] + merid[r + 1]) for r in range(rows + 1)]
    faces[0] = jnp.where(band == 0, 0.0, faces[0])
    faces[rows] = jnp.where(band == bands - 1, 0.0, faces[rows])
    ahead = [jnp.maximum(f, 0.0) for f in faces]
    back = [jnp.minimum(f, 0.0) for f in faces]
    for r in range(rows):
        u = frecv[2 * r]
        face = 0.5 * (u + pltpu.roll(u, 127, 1))
        west_p, west_m = jnp.maximum(face, 0.0), jnp.minimum(face, 0.0)
        face = pltpu.roll(face, 127, 1)
        east_p, east_m = jnp.maximum(face, 0.0), jnp.minimum(face, 0.0)
        centre = 1.0 - (east_p - west_m) - (ahead[r + 1] - back[r])
        for n, (a, b) in enumerate(((centre, -east_m), (west_p, -back[r + 1]), (ahead[r], zero))):
            at = 16 * (r % 8)
            turn[n, r // 8, at : at + 8, :] = jnp.where(low, a, pltpu.roll(b, 64, 1))
            turn[n, r // 8, at + 8 : at + 16, :] = jnp.where(low, pltpu.roll(a, 64, 1), b)
    for n in range(3):
        for octet in range(octets):
            coefs[n, octet] = turn[n, octet].T

    load.wait()
    for copy in edges:
        copy.wait_recv()

    own = lax.div(lane, LEV) == sub

    def expand(n, octet, place):
        x = coefs[n, octet, pl.ds(place, 8, stride=0), :]
        x = jnp.where(own, x, 0.0)
        for turnby in (64, 32, 16):
            x = x + pltpu.roll(x, turnby, 1)
        return x

    modes_width = width // MOMENTS

    parts = modes_width // 128

    def advect(j, buf):
        places = [(0, j), (0, 64 + j), (1, j), (1, 64 + j), (2, j)]
        stencil = [[expand(n, octet, place) for n, place in places] for octet in range(octets)]
        for part in range(parts):
            for k in range(MOMENTS):
                lanes = pl.ds(k * modes_width + part * 128, 128)
                q = [tbuf[j + 1, 8 * o : 8 * o + 8, lanes] for o in range(octets)]
                north_row = jnp.broadcast_to(north_buf[j, :, lanes], (8, 128))
                south_row = jnp.broadcast_to(south_buf[j, :, lanes], (8, 128))
                down = [pltpu.roll(a, 7, 0) for a in q] + [north_row]
                up = [south_row] + [pltpu.roll(a, 1, 0) for a in q]
                for o in range(octets):
                    c, ce, cw, cn, cs = stencil[o]
                    above = jnp.where(sub < 7, down[o], down[o + 1])
                    below = jnp.where(sub > 0, up[o + 1], up[o])
                    octet_rows = pl.ds(8 * o, 8)
                    value = c * q[o] + ce * tbuf[j + 2, octet_rows, lanes] + cw * tbuf[j, octet_rows, lanes]
                    buf[part, o, k] = value + cn * above + cs * below

    def produce(j, buf):
        for part in range(parts):
            for o in range(octets):
                moments = [buf[part, o, k] for k in range(MOMENTS)]
                for k, value in enumerate(moment_sources(moments, rates[0, part], rates[1, part])):
                    out_ref[j, 8 * o : 8 * o + 8, pl.ds(k * modes_width + part * 128, 128)] = value

    for copy in row_copies(groups, 0, 1):
        copy.wait_recv()
    advect(0, even)

    @pl.loop(0, groups)
    def _(g):
        for copy in group_copies(g):
            copy.wait_recv()
        for k in range(GROUP):
            now, later = (even, odd) if k % 2 == 0 else (odd, even)
            advect(GROUP * g + k + 1, later)
            produce(GROUP * g + k, now)

    produce(cols - 1, even)

    each(1, lambda k: wind_copy(k).wait_send())
    each(1, lambda k: back_copy(k).wait_send())

    @pl.when(me == last_unit)
    def _():
        each(0, lambda k: beyond_copy(k, units, north).wait_send())

    @pl.when(me == 1)
    def _():
        each(0, lambda k: beyond_copy(k, units + 1, south).wait_send())

    for copy in edges:
        copy.wait_send()

    for copy in row_copies(groups, 0, 1):
        copy.wait_send()

    @pl.loop(0, groups)
    def _(g):
        for copy in group_copies(g):
            copy.wait_send()


def local(bands, sectors, tracers, winds, row_mask, coag_rate, growth_rate):
    rows, cols, width = tracers.shape
    lines = jnp.asarray(filter_lines(sectors, cols))
    f32, bf16 = jnp.float32, jnp.bfloat16
    dma = pltpu.SemaphoreType.DMA
    groups = (cols - 1) // GROUP
    stage = (width // MOMENTS // 128, rows // 8, MOMENTS, 8, 128)
    anywhere = pl.BlockSpec(memory_space=pltpu.HBM)
    scalars = pl.BlockSpec(memory_space=pltpu.SMEM)
    out = pl.pallas_call(
        functools.partial(kernel, bands, sectors),
        out_shape=pltpu.VMEM((cols, rows, width), f32),
        in_specs=[anywhere, scalars, scalars, scalars, pl.BlockSpec(memory_space=pltpu.VMEM), anywhere],
        out_specs=pl.BlockSpec(memory_space=pltpu.VMEM),
        scratch_shapes=[
            pltpu.VMEM((sectors, 128), f32),
            pltpu.VMEM((sectors, 8, 128), f32),
            pltpu.VMEM((sectors, 8, 128), f32),
            pltpu.VMEM((sectors, 8, 128), f32),
            pltpu.VMEM((sectors + 2, 8, 128), f32),
            pltpu.VMEM((8 * sectors, 64 * sectors), bf16),
            pltpu.VMEM((64 * sectors, 256), bf16),
            pltpu.VMEM((64 * sectors, 256), bf16),
            pltpu.VMEM((3, rows // 8, 128, 128), f32),
            pltpu.VMEM((3, rows // 8, 128, 128), f32),
            pltpu.VMEM((2, 2, 8, 128), f32),
            pltpu.VMEM((cols + 2, rows, width), f32),
            pltpu.VMEM((cols, 1, width), f32),
            pltpu.VMEM((cols, 1, width), f32),
            pltpu.VMEM(stage, f32),
            pltpu.VMEM(stage, f32),
            dma, dma,
            dma((sectors,)), dma((sectors,)), dma((sectors,)), dma((sectors + 2,)),
            dma((2,)), dma((2,)), dma((2, groups + 1)), dma((2, groups + 1)), dma((sectors,)),
        ],
        compiler_params=pltpu.CompilerParams(collective_id=0, has_side_effects=True, vmem_limit_bytes=67043328 - 4 * cols * rows * width),
        name="transport",
    )(lines, row_mask, coag_rate, growth_rate, jnp.transpose(winds, (0, 2, 1)), jnp.transpose(tracers, (1, 0, 2)))
    return jnp.transpose(out, (1, 0, 2))


def solution(mesh):
    bands, sectors = mesh.shape["lat"], mesh.shape["lon"]
    return jax.shard_map(
        functools.partial(local, bands, sectors),
        mesh=mesh,
        in_specs=(P("lat", "lon", None), P("lat", "lon", None), P("lat"), P(), P()),
        out_specs=P("lat", "lon", None),
        check_vma=False,
    )
```

```python
import functools
import math

import jax
import jax.numpy as jnp
import numpy as np
from jax import lax
from jax.experimental import pallas as pl
from jax.experimental.pallas import tpu as pltpu
from jax.sharding import PartitionSpec as P

NLON = 1440
GLOBE_ROWS = 720
LEV = 16
MODES = 16
MOMENTS = 6
FILTER_ROWS = 48
GROUP = 4
MESH = pl.DeviceIdType.MESH

POLY = (
    0.5000000260258313,
    0.577346917369578,
    -0.11103851124670026,
    0.052841409139758516,
    -0.03023539756350864,
    0.016047280362516254,
    -0.0060893456734267045,
    0.0011276362373084019,
)


def filter_lines(sectors, cols):
    rows = np.arange(FILTER_ROWS)
    angles = (-90.0 + 180.0 * (rows + 0.5) / GLOBE_ROWS) * (math.pi / 180.0)
    cosines = np.cos(angles)[:, None]
    sines = np.sin(np.arange(NLON // 2 + 1) * (math.pi / NLON))[None, :]
    factor = cosines / np.maximum(math.cos(math.pi / 4.0) * sines, cosines)
    kernel = np.fft.irfft(factor, n=NLON, axis=1)
    lane = np.arange(128)
    shift = np.where(lane < 64, lane, lane - 128)
    place = (cols * np.arange(sectors)[:, None] - 1 + shift[None, :]) % NLON
    return kernel[:, place].astype(np.float32)


def split_two(x):
    high = x.astype(jnp.bfloat16)
    return high, (x - high.astype(jnp.float32)).astype(jnp.bfloat16)


def positive_root(x):
    return x * lax.rsqrt(x)


def moment_sources(moments, coag, growth):
    m0, m1, m2, m3, m4, m5 = moments
    inv0 = 1.0 / m0
    a0 = m1 * inv0
    s1 = m2 - a0 * m1
    s2 = m3 - a0 * m2
    s3 = m4 - a0 * m3
    s4 = m5 - a0 * m4
    inv1 = 1.0 / s1
    r21 = s2 * inv1
    a1 = r21 - a0
    b1 = s1 * inv0
    t2 = s3 - a1 * s2 - b1 * m2
    t3 = s4 - a1 * s3 - b1 * m3
    a2 = t3 * (1.0 / t2) - r21
    b2 = t2 * inv1
    d1, d2 = a1 - a0, a2 - a0
    c = (d1 + d2) * (1.0 / 3.0)
    e2 = d1 * d2 - (b1 + b2)
    cc = c * c
    p2 = cc - (1.0 / 3.0) * e2
    inv_p = lax.rsqrt(p2)
    p = p2 * inv_p
    half_h = c * (0.5 * cc - 0.25 * e2) - 0.25 * (b1 * d2)
    half_h = half_h * (inv_p * (inv_p * inv_p))
    u = positive_root(jnp.clip(0.5 + half_h, 1e-30, 1.0))
    cosine = POLY[-1] * u + POLY[-2]
    for coef in POLY[-3::-1]:
        cosine = cosine * u + coef
    sine = positive_root(jnp.maximum(1.0 - cosine * cosine, 1e-30))
    along, across = p * cosine, (math.sqrt(3.0) * p) * sine
    rest = c - along
    ys = (c + (along + along), rest + across, rest - across)
    xs = [y + a0 for y in ys]
    gaps = (ys[0] - ys[1], ys[0] - ys[2], ys[1] - ys[2])
    dens = (gaps[0] * gaps[1], -gaps[0] * gaps[2], gaps[1] * gaps[2])
    ws, shares = [], []
    for i, j, k in ((0, 1, 2), (1, 0, 2), (2, 0, 1)):
        above = 1.0 + xs[i]
        share = (s1 + m0 * (ys[j] * ys[k])) / (dens[i] * above)
        ws.append(share * above)
        shares.append(share)
    vs = [x * x * x for x in xs]
    cw = [w * coag for w in ws]
    wv = [ws[i] * vs[i] for i in range(3)]
    diag = [cw[i] * wv[i] for i in range(3)]
    q7 = [wv[i] * (vs[i] * xs[i]) for i in range(3)]
    q8 = [q7[i] * xs[i] for i in range(3)]
    higher = (m3, m4, m5, None, q7[0] + q7[1] + q7[2], q8[0] + q8[1] + q8[2])
    pairs, roots, joins = [], [], []
    for i, j in ((0, 1), (0, 2), (1, 2)):
        joined = vs[i] + vs[j]
        roots.append(jnp.exp2(jnp.log(joined) * (math.log2(math.e) / 3.0)))
        pairs.append(cw[i] * ws[j] * joined)
        joins.append(joined)
    cm0, cm3 = coag * m0, coag * m3
    out = [m0 - cm0 * m3]
    grown = shares[0] + shares[1] + shares[2]
    first = pairs
    for k in range(1, MOMENTS):
        pairs = [pairs[i] * roots[i] for i in range(3)]
        diag = [diag[i] * xs[i] for i in range(3)]
        total = moments[k] + (float(k) * growth) * grown
        grown = moments[k - 1] - grown
        if k == 3:
            left = [pairs[i] - first[i] * joins[i] for i in range(3)]
            total = total + (left[0] + left[1] + left[2])
        else:
            total = total + (pairs[0] + pairs[1] + pairs[2]) - (cm0 * higher[k] + cm3 * moments[k])
            total = total + 2.0 ** (k / 3.0) * (diag[0] + diag[1] + diag[2])
        out.append(total)
    return out


def kernel(
    bands, sectors, lines_ref, mask_ref, coag_ref, growth_ref, winds_ref, tracers_ref, out_ref,
    line_buf, wsend, wrecv, fsend, frecv, wide, table_h, table_l, turn, coefs, rates,
    tbuf, south_buf, north_buf, even, odd,
    line_sem, load_sem, w_send, w_recv, f_send, f_recv, edge_send, edge_recv, row_send, row_recv, v_send,
):
    band, me = lax.axis_index("lat"), lax.axis_index("lon")
    north, south = lax.rem(band + 1, bands), lax.rem(band + bands - 1, bands)
    east, west = lax.rem(me + 1, sectors), lax.rem(me + sectors - 1, sectors)
    rows, channels, cols = winds_ref.shape
    width = tracers_ref.shape[-1]
    octets = rows // 8
    lane = lax.broadcasted_iota(jnp.int32, (8, 128), 1)
    sub = lax.broadcasted_iota(jnp.int32, (8, 128), 0)
    low = lane < 64

    barrier = pltpu.get_barrier_semaphore()

    def greet(k, carry):
        pl.semaphore_signal(barrier, inc=1, device_id=(band, lax.rem(me + k, sectors)), device_id_type=MESH)
        return carry

    lax.fori_loop(1, sectors, greet, 0)
    for other in (north, south):
        pl.semaphore_signal(barrier, inc=1, device_id=(other, me), device_id_type=MESH)
    pl.semaphore_signal(barrier, inc=1, device_id=(north, 1), device_id_type=MESH)
    pl.semaphore_signal(barrier, inc=1, device_id=(south, sectors - 1), device_id_type=MESH)

    unit_row = lax.div(me, 2)
    line = jnp.minimum(band * rows + unit_row, FILTER_ROWS - 1)
    line_copy = pltpu.make_async_copy(lines_ref.at[line], line_buf, line_sem)
    line_copy.start()
    load = pltpu.make_async_copy(tracers_ref, tbuf.at[pl.ds(1, cols)], load_sem)
    load.start()

    for unit in range(2 * rows):
        wsend[unit] = jnp.zeros((8, 128), jnp.float32)
        for g in range(2):
            start = 16 * (unit % 2) + 8 * g
            wsend[unit, :, 64 * g : 64 * g + cols] = winds_ref[unit // 2, start : start + 8, :]
    for half in range(2):
        c = jnp.zeros((8, 128), jnp.float32)
        g = jnp.zeros((8, 128), jnp.float32)
        for mode in range(8):
            here = lax.div(lane, LEV) == mode
            c = jnp.where(here, coag_ref[8 * half + mode], c)
            g = jnp.where(here, growth_ref[8 * half + mode], g)
        rates[0, half] = c
        rates[1, half] = g

    line_copy.wait()
    filtered = mask_ref[unit_row] > 0
    for k in range(sectors):
        parts = []
        for side in range(2):
            e = (side - k) % sectors
            values = line_buf[e : e + 1, :]
            unit_line = jnp.zeros((1, 128), jnp.float32)
            for x in range(128):
                if (cols * e - 1 + (x if x < 64 else x - 128)) % NLON == 0:
                    unit_line = jnp.where(lax.broadcasted_iota(jnp.int32, (1, 128), 1) == x, 1.0, unit_line)
            values = jnp.where(filtered, values, unit_line)
            parts.append(pltpu.roll(jnp.broadcast_to(values, (64, 128)), 64 * side, 1, stride=1, stride_axis=0))
        left = lax.broadcasted_iota(jnp.int32, (64, 128), 1) < 64
        high, rest = split_two(jnp.where(left, parts[0], parts[1]))
        for at, lanes in ((64 * k, 0), (64 * ((k + 2) % sectors), 128)):
            table_h[at : at + 64, lanes : lanes + 128] = high
            table_l[at : at + 64, lanes : lanes + 128] = rest

    extra = jnp.where(jnp.logical_or(me == 1, me == sectors - 1), sectors, 0)
    pl.semaphore_wait(barrier, sectors + 1 + extra)

    def wind_copy(k):
        other = lax.rem(me + k, sectors)
        return pltpu.make_async_remote_copy(
            src_ref=wsend.at[other], dst_ref=wrecv.at[me], send_sem=w_send.at[other], recv_sem=w_recv.at[me],
            device_id=(band, other), device_id_type=MESH,
        )

    def wind_start(k, carry):
        wind_copy(k).start()
        return carry

    for k in sorted(range(1, sectors), key=lambda k: abs(k % 16 - 8)):
        wind_copy(k).start()
    wrecv[me] = wsend[me]

    edges = [
        pltpu.make_async_remote_copy(
            src_ref=tracers_ref.at[cols - 1], dst_ref=tbuf.at[0], send_sem=edge_send.at[0], recv_sem=edge_recv.at[0],
            device_id=(band, east), device_id_type=MESH,
        ),
        pltpu.make_async_remote_copy(
            src_ref=tracers_ref.at[0], dst_ref=tbuf.at[cols + 1], send_sem=edge_send.at[1], recv_sem=edge_recv.at[1],
            device_id=(band, west), device_id_type=MESH,
        ),
    ]
    for copy in edges:
        copy.start()

    groups = (cols - 1) // GROUP

    def row_copies(slot, start, size):
        here = pl.ds(start, size)
        return [
            pltpu.make_async_remote_copy(
                src_ref=tracers_ref.at[here, pl.ds(row, 1), :], dst_ref=dst.at[here], send_sem=row_send.at[side, slot],
                recv_sem=row_recv.at[side, slot], device_id=(target, me), device_id_type=MESH,
            )
            for side, (row, dst, target) in enumerate(((rows - 1, south_buf, north), (0, north_buf, south)))
        ]

    def group_copies(g):
        return row_copies(g, GROUP * g + 1, GROUP)

    def wind_wait(k, carry):
        other = lax.rem(me + k, sectors)
        pltpu.make_async_remote_copy(
            src_ref=wsend.at[me], dst_ref=wrecv.at[other], send_sem=w_send.at[other], recv_sem=w_recv.at[other],
            device_id=(band, other), device_id_type=MESH,
        ).wait_recv()
        return carry

    lax.fori_loop(1, sectors, wind_wait, 0)

    pairs, quads = sectors // 2, sectors // 4
    for q in range(pairs):
        one, two = wrecv[2 * q], wrecv[2 * q + 1]
        block = jnp.concatenate(
            [jnp.where(low, one, pltpu.roll(two, 64, 1)), jnp.where(low, pltpu.roll(one, 64, 1), two)], axis=0
        )
        high, rest = split_two(block)
        for p in range(quads):
            at = 128 * ((q - 2 * p) % pairs)
            wide[16 * p : 16 * p + 16, at : at + 128] = high
            wide[16 * (quads + p) : 16 * (quads + p) + 16, at : at + 128] = rest
    both = jnp.dot(wide[...], table_h[...], preferred_element_type=jnp.float32)
    rest = jnp.dot(wide[0 : 16 * quads, :], table_l[...], preferred_element_type=jnp.float32)
    smooth = both[0 : 16 * quads] + (both[16 * quads :] + rest)
    for p in range(pairs):
        at, lanes = 16 * (p // 2), 128 * (p % 2)
        one, two = smooth[at : at + 8, lanes : lanes + 128], smooth[at + 8 : at + 16, lanes : lanes + 128]
        fsend[2 * p] = jnp.where(low, one, pltpu.roll(two, 64, 1))
        fsend[2 * p + 1] = jnp.where(low, pltpu.roll(one, 64, 1), two)

    units = 2 * rows
    last_unit = units - 1

    def back_copy(k):
        other = lax.rem(me + k, sectors)
        return pltpu.make_async_remote_copy(
            src_ref=fsend.at[other], dst_ref=frecv.at[me], send_sem=f_send.at[other], recv_sem=f_recv.at[me],
            device_id=(band, other), device_id_type=MESH,
        )

    def beyond_copy(k, slot, target):
        other = lax.rem(me + k, sectors)
        return pltpu.make_async_remote_copy(
            src_ref=fsend.at[other], dst_ref=frecv.at[slot], send_sem=v_send.at[other], recv_sem=f_recv.at[slot],
            device_id=(target, other), device_id_type=MESH,
        )

    def each(start, body):
        def step(k, carry):
            body(k)
            return carry

        lax.fori_loop(start, sectors, step, 0)

    @pl.when(me == last_unit)
    def _():
        each(0, lambda k: beyond_copy(k, units, north).start())

    @pl.when(me == 1)
    def _():
        each(0, lambda k: beyond_copy(k, units + 1, south).start())

    for k in sorted(range(1, sectors), key=lambda k: abs(k % 16 - 8)):
        back_copy(k).start()
    frecv[me] = fsend[me]

    for copy in row_copies(groups, 0, 1):
        copy.start()

    @pl.loop(0, groups)
    def _(g):
        for copy in group_copies(g):
            copy.start()


    def arrived(slot):
        pltpu.make_async_remote_copy(
            src_ref=fsend.at[me], dst_ref=frecv.at[slot], send_sem=f_send.at[me], recv_sem=f_recv.at[slot],
            device_id=(band, east), device_id_type=MESH,
        ).wait_recv()

    each(1, lambda k: arrived(lax.rem(me + k, sectors)))
    arrived(units)
    arrived(units + 1)

    zero = jnp.zeros((8, 128), jnp.float32)
    merid = [frecv[units]] + [frecv[2 * r + 1] for r in range(rows)] + [frecv[units + 1]]
    merid = [pltpu.roll(m, 127, 1) for m in merid]
    faces = [0.5 * (merid[r] + merid[r + 1]) for r in range(rows + 1)]
    faces[0] = jnp.where(band == 0, 0.0, faces[0])
    faces[rows] = jnp.where(band == bands - 1, 0.0, faces[rows])
    ahead = [jnp.maximum(f, 0.0) for f in faces]
    back = [jnp.minimum(f, 0.0) for f in faces]
    for r in range(rows):
        u = frecv[2 * r]
        face = 0.5 * (u + pltpu.roll(u, 127, 1))
        west_p, west_m = jnp.maximum(face, 0.0), jnp.minimum(face, 0.0)
        face = pltpu.roll(face, 127, 1)
        east_p, east_m = jnp.maximum(face, 0.0), jnp.minimum(face, 0.0)
        centre = 1.0 - (east_p - west_m) - (ahead[r + 1] - back[r])
        for n, (a, b) in enumerate(((centre, -east_m), (west_p, -back[r + 1]), (ahead[r], zero))):
            at = 16 * (r % 8)
            turn[n, r // 8, at : at + 8, :] = jnp.where(low, a, pltpu.roll(b, 64, 1))
            turn[n, r // 8, at + 8 : at + 16, :] = jnp.where(low, pltpu.roll(a, 64, 1), b)
    for n in range(3):
        for octet in range(octets):
            coefs[n, octet] = turn[n, octet].T

    load.wait()
    for copy in edges:
        copy.wait_recv()

    own = lax.div(lane, LEV) == sub

    def expand(n, octet, place):
        x = coefs[n, octet, pl.ds(place, 8, stride=0), :]
        x = jnp.where(own, x, 0.0)
        for turnby in (64, 32, 16):
            x = x + pltpu.roll(x, turnby, 1)
        return x

    modes_width = width // MOMENTS

    parts = modes_width // 128

    def advect(j, buf):
        places = [(0, j), (0, 64 + j), (1, j), (1, 64 + j), (2, j)]
        stencil = [[expand(n, octet, place) for n, place in places] for octet in range(octets)]
        for part in range(parts):
            for k in range(MOMENTS):
                lanes = pl.ds(k * modes_width + part * 128, 128)
                q = [tbuf[j + 1, 8 * o : 8 * o + 8, lanes] for o in range(octets)]
                north_row = jnp.broadcast_to(north_buf[j, :, lanes], (8, 128))
                south_row = jnp.broadcast_to(south_buf[j, :, lanes], (8, 128))
                down = [pltpu.roll(a, 7, 0) for a in q] + [north_row]
                up = [south_row] + [pltpu.roll(a, 1, 0) for a in q]
                for o in range(octets):
                    c, ce, cw, cn, cs = stencil[o]
                    above = jnp.where(sub < 7, down[o], down[o + 1])
                    below = jnp.where(sub > 0, up[o + 1], up[o])
                    octet_rows = pl.ds(8 * o, 8)
                    value = c * q[o] + ce * tbuf[j + 2, octet_rows, lanes] + cw * tbuf[j, octet_rows, lanes]
                    buf[part, o, k] = value + cn * above + cs * below

    def produce(j, buf):
        for part in range(parts):
            for o in range(octets):
                moments = [buf[part, o, k] for k in range(MOMENTS)]
                for k, value in enumerate(moment_sources(moments, rates[0, part], rates[1, part])):
                    out_ref[j, 8 * o : 8 * o + 8, pl.ds(k * modes_width + part * 128, 128)] = value

    for copy in row_copies(groups, 0, 1):
        copy.wait_recv()
    advect(0, even)

    @pl.loop(0, groups)
    def _(g):
        for copy in group_copies(g):
            copy.wait_recv()
        for k in range(GROUP):
            now, later = (even, odd) if k % 2 == 0 else (odd, even)
            produce(GROUP * g + k, now)
            advect(GROUP * g + k + 1, later)

    produce(cols - 1, even)

    each(1, lambda k: wind_copy(k).wait_send())
    each(1, lambda k: back_copy(k).wait_send())

    @pl.when(me == last_unit)
    def _():
        each(0, lambda k: beyond_copy(k, units, north).wait_send())

    @pl.when(me == 1)
    def _():
        each(0, lambda k: beyond_copy(k, units + 1, south).wait_send())

    for copy in edges:
        copy.wait_send()

    for copy in row_copies(groups, 0, 1):
        copy.wait_send()

    @pl.loop(0, groups)
    def _(g):
        for copy in group_copies(g):
            copy.wait_send()


def local(bands, sectors, tracers, winds, row_mask, coag_rate, growth_rate):
    rows, cols, width = tracers.shape
    lines = jnp.asarray(filter_lines(sectors, cols))
    f32, bf16 = jnp.float32, jnp.bfloat16
    dma = pltpu.SemaphoreType.DMA
    groups = (cols - 1) // GROUP
    stage = (width // MOMENTS // 128, rows // 8, MOMENTS, 8, 128)
    anywhere = pl.BlockSpec(memory_space=pltpu.HBM)
    scalars = pl.BlockSpec(memory_space=pltpu.SMEM)
    out = pl.pallas_call(
        functools.partial(kernel, bands, sectors),
        out_shape=pltpu.VMEM((cols, rows, width), f32),
        in_specs=[anywhere, scalars, scalars, scalars, pl.BlockSpec(memory_space=pltpu.VMEM), anywhere],
        out_specs=pl.BlockSpec(memory_space=pltpu.VMEM),
        scratch_shapes=[
            pltpu.VMEM((sectors, 128), f32),
            pltpu.VMEM((sectors, 8, 128), f32),
            pltpu.VMEM((sectors, 8, 128), f32),
            pltpu.VMEM((sectors, 8, 128), f32),
            pltpu.VMEM((sectors + 2, 8, 128), f32),
            pltpu.VMEM((8 * sectors, 64 * sectors), bf16),
            pltpu.VMEM((64 * sectors, 256), bf16),
            pltpu.VMEM((64 * sectors, 256), bf16),
            pltpu.VMEM((3, rows // 8, 128, 128), f32),
            pltpu.VMEM((3, rows // 8, 128, 128), f32),
            pltpu.VMEM((2, 2, 8, 128), f32),
            pltpu.VMEM((cols + 2, rows, width), f32),
            pltpu.VMEM((cols, 1, width), f32),
            pltpu.VMEM((cols, 1, width), f32),
            pltpu.VMEM(stage, f32),
            pltpu.VMEM(stage, f32),
            dma, dma,
            dma((sectors,)), dma((sectors,)), dma((sectors,)), dma((sectors + 2,)),
            dma((2,)), dma((2,)), dma((2, groups + 1)), dma((2, groups + 1)), dma((sectors,)),
        ],
        compiler_params=pltpu.CompilerParams(collective_id=0, has_side_effects=True, vmem_limit_bytes=67043328 - 4 * cols * rows * width),
        name="transport",
    )(lines, row_mask, coag_rate, growth_rate, jnp.transpose(winds, (0, 2, 1)), jnp.transpose(tracers, (1, 0, 2)))
    return jnp.transpose(out, (1, 0, 2))


def solution(mesh):
    bands, sectors = mesh.shape["lat"], mesh.shape["lon"]
    return jax.shard_map(
        functools.partial(local, bands, sectors),
        mesh=mesh,
        in_specs=(P("lat", "lon", None), P("lat", "lon", None), P("lat"), P(), P()),
        out_specs=P("lat", "lon", None),
        check_vma=False,
    )
```

```python
import functools
import math

import jax
import jax.numpy as jnp
import numpy as np
from jax import lax
from jax.experimental import pallas as pl
from jax.experimental.pallas import tpu as pltpu
from jax.sharding import PartitionSpec as P

NLON = 1440
GLOBE_ROWS = 720
LEV = 16
MODES = 16
MOMENTS = 6
FILTER_ROWS = 48
GROUP = 4
MESH = pl.DeviceIdType.MESH

POLY = (
    0.5000000260258313,
    0.577346917369578,
    -0.11103851124670026,
    0.052841409139758516,
    -0.03023539756350864,
    0.016047280362516254,
    -0.0060893456734267045,
    0.0011276362373084019,
)


def filter_lines(sectors, cols):
    rows = np.arange(FILTER_ROWS)
    angles = (-90.0 + 180.0 * (rows + 0.5) / GLOBE_ROWS) * (math.pi / 180.0)
    cosines = np.cos(angles)[:, None]
    sines = np.sin(np.arange(NLON // 2 + 1) * (math.pi / NLON))[None, :]
    factor = cosines / np.maximum(math.cos(math.pi / 4.0) * sines, cosines)
    kernel = np.fft.irfft(factor, n=NLON, axis=1)
    lane = np.arange(128)
    shift = np.where(lane < 64, lane, lane - 128)
    place = (cols * np.arange(sectors)[:, None] - 1 + shift[None, :]) % NLON
    return kernel[:, place].astype(np.float32)


def split_two(x):
    high = x.astype(jnp.bfloat16)
    return high, (x - high.astype(jnp.float32)).astype(jnp.bfloat16)


def positive_root(x):
    return x * lax.rsqrt(x)


def moment_sources(moments, coag, growth):
    m0, m1, m2, m3, m4, m5 = moments
    inv0 = 1.0 / m0
    a0 = m1 * inv0
    s1 = m2 - a0 * m1
    s2 = m3 - a0 * m2
    s3 = m4 - a0 * m3
    s4 = m5 - a0 * m4
    inv1 = 1.0 / s1
    r21 = s2 * inv1
    a1 = r21 - a0
    b1 = s1 * inv0
    t2 = s3 - a1 * s2 - b1 * m2
    t3 = s4 - a1 * s3 - b1 * m3
    a2 = t3 * (1.0 / t2) - r21
    b2 = t2 * inv1
    d1, d2 = a1 - a0, a2 - a0
    c = (d1 + d2) * (1.0 / 3.0)
    e2 = d1 * d2 - (b1 + b2)
    cc = c * c
    p2 = cc - (1.0 / 3.0) * e2
    inv_p = lax.rsqrt(p2)
    p = p2 * inv_p
    half_h = c * (0.5 * cc - 0.25 * e2) - 0.25 * (b1 * d2)
    half_h = half_h * (inv_p * (inv_p * inv_p))
    u = positive_root(jnp.clip(0.5 + half_h, 1e-30, 1.0))
    cosine = POLY[-1] * u + POLY[-2]
    for coef in POLY[-3::-1]:
        cosine = cosine * u + coef
    sine = positive_root(jnp.maximum(1.0 - cosine * cosine, 1e-30))
    along, across = p * cosine, (math.sqrt(3.0) * p) * sine
    rest = c - along
    ys = (c + (along + along), rest + across, rest - across)
    xs = [y + a0 for y in ys]
    above = [1.0 + x for x in xs]
    wide = ys[0] - ys[2]
    top = (s1 + m0 * (ys[1] * ys[2])) / ((ys[0] - ys[1]) * (wide * above[0]))
    low = (s1 + m0 * (ys[0] * ys[1])) / ((ys[1] - ys[2]) * (wide * above[2]))
    w_top, w_low = top * above[0], low * above[2]
    w_mid = m0 - (w_top + w_low)
    ws, shares = (w_top, w_mid, w_low), (top, w_mid / above[1], low)
    vs = [x * x * x for x in xs]
    cw = [w * coag for w in ws]
    wv = [ws[i] * vs[i] for i in range(3)]
    diag = [cw[i] * wv[i] for i in range(3)]
    q7 = [wv[i] * (vs[i] * xs[i]) for i in range(3)]
    q8 = [q7[i] * xs[i] for i in range(3)]
    higher = (m3, m4, m5, None, q7[0] + q7[1] + q7[2], q8[0] + q8[1] + q8[2])
    pairs, roots, joins = [], [], []
    for i, j in ((0, 1), (0, 2), (1, 2)):
        joined = vs[i] + vs[j]
        roots.append(jnp.exp(jnp.log(joined) * (1.0 / 3.0)))
        pairs.append(cw[i] * ws[j] * joined)
        joins.append(joined)
    cm0, cm3 = coag * m0, coag * m3
    out = [m0 - cm0 * m3]
    grown = shares[0] + shares[1] + shares[2]
    first = pairs
    for k in range(1, MOMENTS):
        pairs = [pairs[i] * roots[i] for i in range(3)]
        diag = [diag[i] * xs[i] for i in range(3)]
        total = moments[k] + growth[k - 1] * grown
        grown = moments[k - 1] - grown
        if k == 3:
            left = [pairs[i] - first[i] * joins[i] for i in range(3)]
            total = total + (left[0] + left[1] + left[2])
        else:
            total = total + (pairs[0] + pairs[1] + pairs[2]) - (cm0 * higher[k] + cm3 * moments[k])
            total = total + 2.0 ** (k / 3.0) * (diag[0] + diag[1] + diag[2])
        out.append(total)
    return out


def kernel(
    bands, sectors, lines_ref, mask_ref, coag_ref, growth_ref, winds_ref, tracers_ref, out_ref,
    line_buf, wsend, wrecv, fsend, frecv, wide, table_h, table_l, turn, coefs, rates,
    tbuf, south_buf, north_buf, even, odd,
    line_sem, load_sem, w_send, w_recv, f_send, f_recv, edge_send, edge_recv, row_send, row_recv, v_send,
):
    band, me = lax.axis_index("lat"), lax.axis_index("lon")
    north, south = lax.rem(band + 1, bands), lax.rem(band + bands - 1, bands)
    east, west = lax.rem(me + 1, sectors), lax.rem(me + sectors - 1, sectors)
    rows, channels, cols = winds_ref.shape
    width = tracers_ref.shape[-1]
    octets = rows // 8
    lane = lax.broadcasted_iota(jnp.int32, (8, 128), 1)
    sub = lax.broadcasted_iota(jnp.int32, (8, 128), 0)
    low = lane < 64

    barrier = pltpu.get_barrier_semaphore()

    def greet(k, carry):
        pl.semaphore_signal(barrier, inc=1, device_id=(band, lax.rem(me + k, sectors)), device_id_type=MESH)
        return carry

    lax.fori_loop(1, sectors, greet, 0)
    for other in (north, south):
        pl.semaphore_signal(barrier, inc=1, device_id=(other, me), device_id_type=MESH)
    pl.semaphore_signal(barrier, inc=1, device_id=(north, 1), device_id_type=MESH)
    pl.semaphore_signal(barrier, inc=1, device_id=(south, sectors - 1), device_id_type=MESH)

    unit_row = lax.div(me, 2)
    line = jnp.minimum(band * rows + unit_row, FILTER_ROWS - 1)
    line_copy = pltpu.make_async_copy(lines_ref.at[line], line_buf, line_sem)
    line_copy.start()
    load = pltpu.make_async_copy(tracers_ref, tbuf.at[pl.ds(1, cols)], load_sem)
    load.start()

    for unit in range(2 * rows):
        wsend[unit] = jnp.zeros((8, 128), jnp.float32)
        for g in range(2):
            start = 16 * (unit % 2) + 8 * g
            wsend[unit, :, 64 * g : 64 * g + cols] = winds_ref[unit // 2, start : start + 8, :]
    for half in range(2):
        c = jnp.zeros((8, 128), jnp.float32)
        g = jnp.zeros((8, 128), jnp.float32)
        for mode in range(8):
            here = lax.div(lane, LEV) == mode
            c = jnp.where(here, coag_ref[8 * half + mode], c)
            g = jnp.where(here, growth_ref[8 * half + mode], g)
        rates[0, half] = c
        for k in range(1, MOMENTS):
            rates[k, half] = float(k) * g

    line_copy.wait()
    filtered = mask_ref[unit_row] > 0
    for k in range(sectors):
        parts = []
        for side in range(2):
            e = (side - k) % sectors
            values = line_buf[e : e + 1, :]
            unit_line = jnp.zeros((1, 128), jnp.float32)
            for x in range(128):
                if (cols * e - 1 + (x if x < 64 else x - 128)) % NLON == 0:
                    unit_line = jnp.where(lax.broadcasted_iota(jnp.int32, (1, 128), 1) == x, 1.0, unit_line)
            values = jnp.where(filtered, values, unit_line)
            parts.append(pltpu.roll(jnp.broadcast_to(values, (64, 128)), 64 * side, 1, stride=1, stride_axis=0))
        left = lax.broadcasted_iota(jnp.int32, (64, 128), 1) < 64
        high, rest = split_two(jnp.where(left, parts[0], parts[1]))
        for at, lanes in ((64 * k, 0), (64 * ((k + 2) % sectors), 128)):
            table_h[at : at + 64, lanes : lanes + 128] = high
            table_l[at : at + 64, lanes : lanes + 128] = rest

    extra = jnp.where(jnp.logical_or(me == 1, me == sectors - 1), sectors, 0)
    pl.semaphore_wait(barrier, sectors + 1 + extra)

    def wind_copy(k):
        other = lax.rem(me + k, sectors)
        return pltpu.make_async_remote_copy(
            src_ref=wsend.at[other], dst_ref=wrecv.at[me], send_sem=w_send.at[other], recv_sem=w_recv.at[me],
            device_id=(band, other), device_id_type=MESH,
        )

    def wind_start(k, carry):
        wind_copy(k).start()
        return carry

    for k in sorted(range(1, sectors), key=lambda k: abs(k % 16 - 8)):
        wind_copy(k).start()
    wrecv[me] = wsend[me]

    edges = [
        pltpu.make_async_remote_copy(
            src_ref=tracers_ref.at[cols - 1], dst_ref=tbuf.at[0], send_sem=edge_send.at[0], recv_sem=edge_recv.at[0],
            device_id=(band, east), device_id_type=MESH,
        ),
        pltpu.make_async_remote_copy(
            src_ref=tracers_ref.at[0], dst_ref=tbuf.at[cols + 1], send_sem=edge_send.at[1], recv_sem=edge_recv.at[1],
            device_id=(band, west), device_id_type=MESH,
        ),
    ]
    for copy in edges:
        copy.start()

    groups = (cols - 1) // GROUP

    def row_copies(slot, start, size):
        here = pl.ds(start, size)
        return [
            pltpu.make_async_remote_copy(
                src_ref=tracers_ref.at[here, pl.ds(row, 1), :], dst_ref=dst.at[here], send_sem=row_send.at[side, slot],
                recv_sem=row_recv.at[side, slot], device_id=(target, me), device_id_type=MESH,
            )
            for side, (row, dst, target) in enumerate(((rows - 1, south_buf, north), (0, north_buf, south)))
        ]

    def group_copies(g):
        return row_copies(g, GROUP * g + 1, GROUP)

    def wind_wait(k, carry):
        other = lax.rem(me + k, sectors)
        pltpu.make_async_remote_copy(
            src_ref=wsend.at[me], dst_ref=wrecv.at[other], send_sem=w_send.at[other], recv_sem=w_recv.at[other],
            device_id=(band, other), device_id_type=MESH,
        ).wait_recv()
        return carry

    lax.fori_loop(1, sectors, wind_wait, 0)

    pairs, quads = sectors // 2, sectors // 4
    for q in range(pairs):
        one, two = wrecv[2 * q], wrecv[2 * q + 1]
        block = jnp.concatenate(
            [jnp.where(low, one, pltpu.roll(two, 64, 1)), jnp.where(low, pltpu.roll(one, 64, 1), two)], axis=0
        )
        high, rest = split_two(block)
        for p in range(quads):
            at = 128 * ((q - 2 * p) % pairs)
            wide[16 * p : 16 * p + 16, at : at + 128] = high
            wide[16 * (quads + p) : 16 * (quads + p) + 16, at : at + 128] = rest
    both = jnp.dot(wide[...], table_h[...], preferred_element_type=jnp.float32)
    rest = jnp.dot(wide[0 : 16 * quads, :], table_l[...], preferred_element_type=jnp.float32)
    smooth = both[0 : 16 * quads] + (both[16 * quads :] + rest)
    for p in range(pairs):
        at, lanes = 16 * (p // 2), 128 * (p % 2)
        one, two = smooth[at : at + 8, lanes : lanes + 128], smooth[at + 8 : at + 16, lanes : lanes + 128]
        fsend[2 * p] = jnp.where(low, one, pltpu.roll(two, 64, 1))
        fsend[2 * p + 1] = jnp.where(low, pltpu.roll(one, 64, 1), two)

    units = 2 * rows
    last_unit = units - 1

    def back_copy(k):
        other = lax.rem(me + k, sectors)
        return pltpu.make_async_remote_copy(
            src_ref=fsend.at[other], dst_ref=frecv.at[me], send_sem=f_send.at[other], recv_sem=f_recv.at[me],
            device_id=(band, other), device_id_type=MESH,
        )

    def beyond_copy(k, slot, target):
        other = lax.rem(me + k, sectors)
        return pltpu.make_async_remote_copy(
            src_ref=fsend.at[other], dst_ref=frecv.at[slot], send_sem=v_send.at[other], recv_sem=f_recv.at[slot],
            device_id=(target, other), device_id_type=MESH,
        )

    def each(start, body):
        def step(k, carry):
            body(k)
            return carry

        lax.fori_loop(start, sectors, step, 0)

    @pl.when(me == last_unit)
    def _():
        each(0, lambda k: beyond_copy(k, units, north).start())

    @pl.when(me == 1)
    def _():
        each(0, lambda k: beyond_copy(k, units + 1, south).start())

    for k in sorted(range(1, sectors), key=lambda k: abs(k % 16 - 8)):
        back_copy(k).start()
    frecv[me] = fsend[me]

    for copy in row_copies(groups, 0, 1):
        copy.start()

    @pl.loop(0, groups)
    def _(g):
        for copy in group_copies(g):
            copy.start()


    def arrived(slot):
        pltpu.make_async_remote_copy(
            src_ref=fsend.at[me], dst_ref=frecv.at[slot], send_sem=f_send.at[me], recv_sem=f_recv.at[slot],
            device_id=(band, east), device_id_type=MESH,
        ).wait_recv()

    each(1, lambda k: arrived(lax.rem(me + k, sectors)))
    arrived(units)
    arrived(units + 1)

    zero = jnp.zeros((8, 128), jnp.float32)
    merid = [frecv[units]] + [frecv[2 * r + 1] for r in range(rows)] + [frecv[units + 1]]
    merid = [pltpu.roll(m, 127, 1) for m in merid]
    faces = [0.5 * (merid[r] + merid[r + 1]) for r in range(rows + 1)]
    faces[0] = jnp.where(band == 0, 0.0, faces[0])
    faces[rows] = jnp.where(band == bands - 1, 0.0, faces[rows])
    ahead = [jnp.maximum(f, 0.0) for f in faces]
    back = [jnp.minimum(f, 0.0) for f in faces]
    for r in range(rows):
        u = frecv[2 * r]
        face = 0.5 * (u + pltpu.roll(u, 127, 1))
        west_p, west_m = jnp.maximum(face, 0.0), jnp.minimum(face, 0.0)
        face = pltpu.roll(face, 127, 1)
        east_p, east_m = jnp.maximum(face, 0.0), jnp.minimum(face, 0.0)
        centre = 1.0 - (east_p - west_m) - (ahead[r + 1] - back[r])
        for n, (a, b) in enumerate(((centre, -east_m), (west_p, -back[r + 1]), (ahead[r], zero))):
            at = 16 * (r % 8)
            turn[n, r // 8, at : at + 8, :] = jnp.where(low, a, pltpu.roll(b, 64, 1))
            turn[n, r // 8, at + 8 : at + 16, :] = jnp.where(low, pltpu.roll(a, 64, 1), b)
    for n in range(3):
        for octet in range(octets):
            coefs[n, octet] = turn[n, octet].T

    load.wait()
    for copy in edges:
        copy.wait_recv()

    own = lax.div(lane, LEV) == sub

    def expand(n, octet, place):
        x = coefs[n, octet, pl.ds(place, 8, stride=0), :]
        x = jnp.where(own, x, 0.0)
        for turnby in (64, 32, 16):
            x = x + pltpu.roll(x, turnby, 1)
        return x

    modes_width = width // MOMENTS

    parts = modes_width // 128

    def advect(j, buf):
        places = [(0, j), (0, 64 + j), (1, j), (1, 64 + j), (2, j)]
        stencil = [[expand(n, octet, place) for n, place in places] for octet in range(octets)]
        for part in range(parts):
            for k in range(MOMENTS):
                lanes = pl.ds(k * modes_width + part * 128, 128)
                q = [tbuf[j + 1, 8 * o : 8 * o + 8, lanes] for o in range(octets)]
                north_row = jnp.broadcast_to(north_buf[j, :, lanes], (8, 128))
                south_row = jnp.broadcast_to(south_buf[j, :, lanes], (8, 128))
                down = [pltpu.roll(a, 7, 0) for a in q] + [north_row]
                up = [south_row] + [pltpu.roll(a, 1, 0) for a in q]
                for o in range(octets):
                    c, ce, cw, cn, cs = stencil[o]
                    above = jnp.where(sub < 7, down[o], down[o + 1])
                    below = jnp.where(sub > 0, up[o + 1], up[o])
                    octet_rows = pl.ds(8 * o, 8)
                    value = c * q[o] + ce * tbuf[j + 2, octet_rows, lanes] + cw * tbuf[j, octet_rows, lanes]
                    buf[part, o, k] = value + cn * above + cs * below

    def produce(j, buf):
        for part in range(parts):
            for o in range(octets):
                moments = [buf[part, o, k] for k in range(MOMENTS)]
                for k, value in enumerate(moment_sources(moments, rates[0, part], [rates[k, part] for k in range(1, MOMENTS)])):
                    out_ref[j, 8 * o : 8 * o + 8, pl.ds(k * modes_width + part * 128, 128)] = value

    for copy in row_copies(groups, 0, 1):
        copy.wait_recv()
    advect(0, even)

    @pl.loop(0, groups)
    def _(g):
        for copy in group_copies(g):
            copy.wait_recv()
        for k in range(GROUP):
            now, later = (even, odd) if k % 2 == 0 else (odd, even)
            produce(GROUP * g + k, now)
            advect(GROUP * g + k + 1, later)

    produce(cols - 1, even)

    each(1, lambda k: wind_copy(k).wait_send())
    each(1, lambda k: back_copy(k).wait_send())

    @pl.when(me == last_unit)
    def _():
        each(0, lambda k: beyond_copy(k, units, north).wait_send())

    @pl.when(me == 1)
    def _():
        each(0, lambda k: beyond_copy(k, units + 1, south).wait_send())

    for copy in edges:
        copy.wait_send()

    for copy in row_copies(groups, 0, 1):
        copy.wait_send()

    @pl.loop(0, groups)
    def _(g):
        for copy in group_copies(g):
            copy.wait_send()


def local(bands, sectors, tracers, winds, row_mask, coag_rate, growth_rate):
    rows, cols, width = tracers.shape
    lines = jnp.asarray(filter_lines(sectors, cols))
    f32, bf16 = jnp.float32, jnp.bfloat16
    dma = pltpu.SemaphoreType.DMA
    groups = (cols - 1) // GROUP
    stage = (width // MOMENTS // 128, rows // 8, MOMENTS, 8, 128)
    anywhere = pl.BlockSpec(memory_space=pltpu.HBM)
    scalars = pl.BlockSpec(memory_space=pltpu.SMEM)
    out = pl.pallas_call(
        functools.partial(kernel, bands, sectors),
        out_shape=pltpu.VMEM((cols, rows, width), f32),
        in_specs=[anywhere, scalars, scalars, scalars, pl.BlockSpec(memory_space=pltpu.VMEM), anywhere],
        out_specs=pl.BlockSpec(memory_space=pltpu.VMEM),
        scratch_shapes=[
            pltpu.VMEM((sectors, 128), f32),
            pltpu.VMEM((sectors, 8, 128), f32),
            pltpu.VMEM((sectors, 8, 128), f32),
            pltpu.VMEM((sectors, 8, 128), f32),
            pltpu.VMEM((sectors + 2, 8, 128), f32),
            pltpu.VMEM((8 * sectors, 64 * sectors), bf16),
            pltpu.VMEM((64 * sectors, 256), bf16),
            pltpu.VMEM((64 * sectors, 256), bf16),
            pltpu.VMEM((3, rows // 8, 128, 128), f32),
            pltpu.VMEM((3, rows // 8, 128, 128), f32),
            pltpu.VMEM((MOMENTS, 2, 8, 128), f32),
            pltpu.VMEM((cols + 2, rows, width), f32),
            pltpu.VMEM((cols, 1, width), f32),
            pltpu.VMEM((cols, 1, width), f32),
            pltpu.VMEM(stage, f32),
            pltpu.VMEM(stage, f32),
            dma, dma,
            dma((sectors,)), dma((sectors,)), dma((sectors,)), dma((sectors + 2,)),
            dma((2,)), dma((2,)), dma((2, groups + 1)), dma((2, groups + 1)), dma((sectors,)),
        ],
        compiler_params=pltpu.CompilerParams(collective_id=0, has_side_effects=True, vmem_limit_bytes=67043328 - 4 * cols * rows * width),
        name="transport",
    )(lines, row_mask, coag_rate, growth_rate, jnp.transpose(winds, (0, 2, 1)), jnp.transpose(tracers, (1, 0, 2)))
    return jnp.transpose(out, (1, 0, 2))


def solution(mesh):
    bands, sectors = mesh.shape["lat"], mesh.shape["lon"]
    return jax.shard_map(
        functools.partial(local, bands, sectors),
        mesh=mesh,
        in_specs=(P("lat", "lon", None), P("lat", "lon", None), P("lat"), P(), P()),
        out_specs=P("lat", "lon", None),
        check_vma=False,
    )
```
